256 devices in a mesh: gx: 64 (over x, z, y_lo), gy: 4 (over y_hi, core).
Axes of the slice: x: 4, y: 4 (y_hi: 2, y_lo: 2; y = y_hi * 2 + y_lo), z: 8, core: 2. Of those that a mesh axis runs over, the one named last changes fastest.
Arguments:
- positions: float32 [3, 2, 128, 8, 128], P(None, None, 'gx', 'gy'), may hold values from 0 to 128, as said below
- charges: float32 [2, 128, 8, 128], P(None, 'gx', 'gy'), may hold values from -6 to 6
- slot_bead_types: int32 [2, 128, 8, 128], P(None, 'gx', 'gy'), may hold values from 0 to 31
- cell_counts: int32 [2, 128, 8], P(None, 'gx', 'gy'), may hold values from 26 to 128, as said below
- features: bfloat16 [2, 128, 8, 128, 128], P(None, 'gx', 'gy'), may hold values from -6 to 6
- radius_table: float32 [32], replicated, may hold values from 0.12 to 0.25
- scale_table: float32 [32], replicated, may hold values from 0.6 to 0.95
- mix_weight: bfloat16 [128, 128], replicated, may hold values from -0.25 to 0.25
- out_weight: float32 [128], replicated, may hold values from -0.5 to 0.5
- targets: float32 [2], replicated, may hold values from -3 to 0
Outputs:
- energies: float32 [2], replicated
- forces: float32 [3, 2, 128, 8, 128], P(None, None, 'gx', 'gy')
- grad_mix: float32 [128, 128], replicated
- grad_out: float32 [128], replicated
- grad_scale: float32 [32], replicated
The draws below stay inside these ranges and needn't reach their ends.
Inputs may be any that keep to these rules, and one draw needn't show every extreme that they name: `positions`: the x and y coordinates of every slot of cell column (i, j) lie in [i, i + 1) and [j, j + 1), z in [0, 8). `cell_counts`: the beads of a cell column fill its first slots; in every frame some cell column holds exactly 128 beads.
All inputs are finite; a program needn't handle non-finite values.
Results may differ from the reference program's by a relative error of at most 0.0029.
Values may be sent and summed in bfloat16 or wider, within the bound.
No kernel may reach another device: no remote copies, remote signals or barrier semaphores. Data moves between devices by JAX's collectives and lax.ppermute only.
A program may use at most 128 MiB of HBM per device.

```python
import math
import jax
import jax.numpy as jnp
from jax import lax

DEVICE_COLUMNS_X = 2
COLUMN_SLOTS = 128
FEATURE_CHANNELS = 128
BEAD_KINDS = 32
FRAME_COUNT = 2
GRID_COLUMNS_X = 128
GRID_COLUMNS_Y = 8


def draw_positions(key, part):
    unit_interval = jax.random.uniform(key, (3, FRAME_COUNT, GRID_COLUMNS_X, GRID_COLUMNS_Y, COLUMN_SLOTS), jnp.float32)
    column_offset_x = jnp.arange(GRID_COLUMNS_X, dtype=jnp.float32)[None, :, None, None]
    base_y = jnp.arange(GRID_COLUMNS_Y, dtype=jnp.float32)[None, None, :, None]
    return jnp.stack([column_offset_x + unit_interval[0], base_y + unit_interval[1], 8.0 * unit_interval[2]], axis=0)


def draw_charges(key, part):
    array_extent = (FRAME_COUNT, GRID_COLUMNS_X, GRID_COLUMNS_Y, COLUMN_SLOTS)
    slot_ramp_values = 0.5 + jnp.arange(GRID_COLUMNS_X, dtype=jnp.float32)[None, :, None, None] / GRID_COLUMNS_X
    core = jnp.clip(jax.random.normal(key, array_extent, jnp.float32), -4.0, 4.0)
    result = core * slot_ramp_values
    return result


def draw_cell_counts(key, part):
    counts_random_key = jax.random.fold_in(key, 11)
    filled_random_key = jax.random.fold_in(key, 23)
    occupancy_counts = jax.random.randint(counts_random_key, (FRAME_COUNT, GRID_COLUMNS_X * GRID_COLUMNS_Y), COLUMN_SLOTS // 5 + 1, COLUMN_SLOTS + 1)
    picked_slots = jax.random.randint(filled_random_key, (FRAME_COUNT, 1), 0, GRID_COLUMNS_X * GRID_COLUMNS_Y)
    filled_column = jnp.arange(GRID_COLUMNS_X * GRID_COLUMNS_Y, dtype=jnp.int32)[None, :] == picked_slots
    return jnp.where(filled_column, COLUMN_SLOTS, occupancy_counts).reshape(FRAME_COUNT, GRID_COLUMNS_X, GRID_COLUMNS_Y).astype(jnp.int32)


def place_ends(entries, key, low, largest):
    index_at = [jax.random.randint(jax.random.fold_in(key, axis), (), 0, length) for axis, length in enumerate(entries.shape)]
    longest = entries.shape.index(max(entries.shape))
    neighbour = index_at[:longest] + [(index_at[longest] + 1) % entries.shape[longest]] + index_at[longest + 1:]
    return entries.at[tuple(index_at)].set(low).at[tuple(neighbour)].set(largest)


def block_levels(stream_key, extent, shards, least, high):
    factor_of = 1.0
    for position, parts in shards:
        draws = jax.random.uniform(jax.random.fold_in(jax.random.fold_in(stream_key, 6), position), (parts,), jnp.float32, least / len(shards), high / len(shards))
        factor_of = factor_of * jnp.repeat(jnp.exp(draws), extent[position] // parts).reshape((-1,) + (1,) * (len(extent) - 1 - position))
    return factor_of


def centred(own_key, shape, deviation, reach, pieces=(), kind=jnp.bfloat16):
    values = jax.random.normal(own_key, shape, jnp.float32) * deviation
    if len(pieces) > 0:
        values = block_levels(own_key, shape, pieces, -0.22, 0.18) * values
    return jnp.clip(values, min=-reach, max=reach).astype(kind)


def setup_inputs(seed: int = 0) -> dict:
    seeds = jax.random.split(jax.random.key(seed), 11)
    positions = draw_positions(jax.random.fold_in(seeds[10], 71), 0)
    charges = draw_charges(jax.random.fold_in(seeds[10], 71), 0)
    slot_bead_types = place_ends(jax.random.randint(seeds[2], (FRAME_COUNT, GRID_COLUMNS_X, GRID_COLUMNS_Y, COLUMN_SLOTS), 0, BEAD_KINDS), jax.random.fold_in(seeds[2], 1), 0, BEAD_KINDS - 1).astype(jnp.int32)
    cell_counts = draw_cell_counts(jax.random.fold_in(seeds[10], 71), 0)
    features = centred(seeds[4], (FRAME_COUNT, GRID_COLUMNS_X, GRID_COLUMNS_Y, COLUMN_SLOTS, FEATURE_CHANNELS), 1.0, 6.0, ((1, 64), (2, 4)))
    radius_table = jnp.clip(jnp.exp(jax.random.uniform(seeds[5], (BEAD_KINDS,), jnp.float32, math.log(0.12), math.log(0.25))), 0.12, 0.25)
    scale_table = jnp.clip(jax.random.uniform(seeds[6], (BEAD_KINDS,), jnp.float32, 0.6, 0.95), 0.6, 0.95)
    mix_weight = centred(seeds[7], (FEATURE_CHANNELS, FEATURE_CHANNELS), (4 * FEATURE_CHANNELS) ** -0.5, 0.25)
    out_weight = centred(seeds[8], (FEATURE_CHANNELS,), FEATURE_CHANNELS ** -0.5, 0.5, (), jnp.float32)
    targets = jnp.clip(jax.random.uniform(seeds[9], (FRAME_COUNT,), jnp.float32, -3.0, 0.0), -3.0, 0.0)
    return {"positions": positions, "charges": charges, "slot_bead_types": slot_bead_types, "cell_counts": cell_counts, "features": features, "radius_table": radius_table, "scale_table": scale_table, "mix_weight": mix_weight, "out_weight": out_weight, "targets": targets}


CUTOFF_SQ = 1.0
GAUSS_WIDTH_SQ = 0.25
SOLVENT_FACTOR = 0.98726
SCREEN_GAIN = 12.0

def smooth_taper(dist_sq):
    inside = jnp.maximum(1.0 - dist_sq / CUTOFF_SQ, 0.0)
    return (inside * inside, -2.0 * inside / CUTOFF_SQ)

def window(ext_cells, shift_x, shift_y, cells_x, cells_y):
    return ext_cells[:, 1 + shift_x:1 + shift_x + cells_x, 1 + shift_y:1 + shift_y + cells_y]

def window_wide(ext_cells, shift_x, shift_y, cells_x, cells_y):
    return ext_cells[1 + shift_x:1 + shift_x + cells_x, 1 + shift_y:1 + shift_y + cells_y]

def distances(own_cells, near_cells):
    offset_vec = own_cells[0:3, :, :, :, None] - near_cells[0:3, :, :, None, :]
    return lax.optimization_barrier(jnp.sum(offset_vec * offset_vec, axis=0))

def pair_push(pair_coef, own_cells, near_cells):
    offset_vec = own_cells[0:3, :, :, :, None] - near_cells[0:3, :, :, None, :]
    return lax.optimization_barrier(jnp.sum(pair_coef[None] * offset_vec, axis=-1))

def pair_mask(own_cells, near_cells, shift_x, shift_y, skip_self):
    mask_pairs = own_cells[6][..., :, None] * near_cells[6][..., None, :]
    if skip_self and shift_x == 0 and (shift_y == 0):
        slot_count = own_cells.shape[3]
        mask_pairs = mask_pairs * (1.0 - jnp.eye(slot_count, dtype=jnp.float32))
    return mask_pairs

def spread(weights, near_feat):
    return jnp.einsum('abij,abjh->abih', weights.astype(jnp.float32), near_feat.astype(jnp.float32))

def pair_inner(left_feat, right_feat):
    return jnp.einsum('abih,abjh->abij', left_feat.astype(jnp.float32), right_feat.astype(jnp.float32))

def back_project(grad_hidden, mix_weight):
    feat_dim = grad_hidden.shape[-1]
    flat_grad = jnp.dot(grad_hidden.reshape(-1, feat_dim), mix_weight.T, preferred_element_type=jnp.float32)
    return flat_grad.reshape(grad_hidden.shape)

def parameter_terms(own_cells, kind_hot, grad_reach, message_low, grad_hidden, grad_corr, hidden_act):
    feat_dim = message_low.shape[-1]
    mix_part = jnp.dot(message_low.reshape(-1, feat_dim).T, grad_hidden.reshape(-1, feat_dim), preferred_element_type=jnp.float32)
    out_part = lax.optimization_barrier(jnp.sum((grad_corr[..., None] * hidden_act).reshape(-1, feat_dim), axis=0))
    scale_part = lax.optimization_barrier(jnp.sum((kind_hot * (own_cells[4] * grad_reach)[None]).reshape(kind_hot.shape[0], -1), axis=1))
    return (mix_part, out_part, scale_part)

def first_pass(own_cells, ext_cells, own_feat, ext_feat):
    cells_x, cells_y = (own_cells.shape[1], own_cells.shape[2])
    descreen = jnp.zeros(own_cells.shape[1:], jnp.float32)
    messages = jnp.zeros(own_feat.shape, jnp.float32)
    for shift_x in (-1, 0, 1):
        for shift_y in (-1, 0, 1):
            near_cells = window(ext_cells, shift_x, shift_y, cells_x, cells_y)
            near_feat = window_wide(ext_feat, shift_x, shift_y, cells_x, cells_y)
            dist_sq = distances(own_cells, near_cells)
            taper_val, taper_slope = smooth_taper(dist_sq)
            mask_pairs = pair_mask(own_cells, near_cells, shift_x, shift_y, True)
            reach_near = near_cells[5][..., None, :]
            rho_own = own_cells[4][..., :, None]
            denom_own = dist_sq + reach_near * reach_near + rho_own * rho_own
            descreen = descreen + lax.optimization_barrier(jnp.sum(mask_pairs * taper_val * reach_near ** 3 / (denom_own * denom_own), axis=-1))
            weights = (mask_pairs * taper_val * jnp.exp(-dist_sq / GAUSS_WIDTH_SQ)).astype(jnp.bfloat16)
            messages = messages + spread(weights, near_feat)
    return (descreen, messages)

def born_radii(own_cells, descreen, message_low, mix_weight, out_weight):
    rho_own = own_cells[4]
    feat_dim = message_low.shape[-1]
    flat_hidden = jnp.dot(message_low.reshape(-1, feat_dim), mix_weight, preferred_element_type=jnp.float32)
    hidden_act = jnp.tanh(flat_hidden).reshape(message_low.shape)
    correction = lax.optimization_barrier(jnp.sum(hidden_act * out_weight, axis=-1))
    tanh_screen = jnp.tanh(SCREEN_GAIN * rho_own * descreen)
    tanh_corr = jnp.tanh(correction)
    born_radius = rho_own * (1.0 + 0.5 * tanh_corr) / (1.0 - 0.8 * tanh_screen)
    return (born_radius, hidden_act, tanh_screen, tanh_corr)

def second_pass(own_cells, ext_cells, born_radius, ext_born):
    cells_x, cells_y = (own_cells.shape[1], own_cells.shape[2])
    energy = jnp.zeros((), jnp.float32)
    grad_born = jnp.zeros(born_radius.shape, jnp.float32)
    direct_grad = jnp.zeros(own_cells[0:3].shape, jnp.float32)
    for shift_x in (-1, 0, 1):
        for shift_y in (-1, 0, 1):
            near_cells = window(ext_cells, shift_x, shift_y, cells_x, cells_y)
            near_born = window(ext_born, shift_x, shift_y, cells_x, cells_y)[0][..., None, :]
            dist_sq = distances(own_cells, near_cells)
            taper_val, taper_slope = smooth_taper(dist_sq)
            mask_pairs = pair_mask(own_cells, near_cells, shift_x, shift_y, False)
            mask_apart = pair_mask(own_cells, near_cells, shift_x, shift_y, True)
            radius_prod = jnp.where(mask_pairs > 0.0, born_radius[..., :, None] * near_born, 1.0)
            decay_term = jnp.exp(-dist_sq / (4.0 * radius_prod))
            reach_sq = dist_sq + radius_prod * decay_term
            reach_len = jnp.sqrt(reach_sq)
            strength = -0.5 * SOLVENT_FACTOR * mask_pairs * own_cells[3][..., :, None] * near_cells[3][..., None, :]
            pair_energy = strength * taper_val / reach_len
            energy = energy + jnp.sum(pair_energy)
            grad_born = grad_born + lax.optimization_barrier(jnp.sum(-pair_energy * decay_term * (1.0 + dist_sq / (4.0 * radius_prod)) * near_born / reach_sq, axis=-1))
            pair_rate = mask_apart * strength * (taper_slope / reach_len - taper_val * (1.0 - 0.25 * decay_term) / (2.0 * reach_len * reach_sq))
            direct_grad = direct_grad + 4.0 * pair_push(pair_rate, own_cells, near_cells)
    return (energy, grad_born, direct_grad)

def radius_backs(own_cells, grad_born, tanh_screen, tanh_corr):
    rho_own = own_cells[4]
    scale_down = 1.0 - 0.8 * tanh_screen
    grad_descreen = SCREEN_GAIN * rho_own * grad_born * rho_own * (1.0 + 0.5 * tanh_corr) * 0.8 * (1.0 - tanh_screen * tanh_screen) / (scale_down * scale_down)
    grad_corr = grad_born * rho_own * 0.5 * (1.0 - tanh_corr * tanh_corr) / scale_down
    return (grad_descreen, grad_corr)

def third_pass(own_cells, ext_cells, grad_descreen, ext_gdesc, grad_message, ext_gmsg, own_feat, ext_feat):
    cells_x, cells_y = (own_cells.shape[1], own_cells.shape[2])
    indirect = jnp.zeros(own_cells[0:3].shape, jnp.float32)
    grad_reach = jnp.zeros(own_cells.shape[1:], jnp.float32)
    for shift_x in (-1, 0, 1):
        for shift_y in (-1, 0, 1):
            near_cells = window(ext_cells, shift_x, shift_y, cells_x, cells_y)
            near_gdesc = window(ext_gdesc, shift_x, shift_y, cells_x, cells_y)[0][..., None, :]
            near_gmsg = window_wide(ext_gmsg, shift_x, shift_y, cells_x, cells_y)
            near_feat = window_wide(ext_feat, shift_x, shift_y, cells_x, cells_y)
            dist_sq = distances(own_cells, near_cells)
            taper_val, taper_slope = smooth_taper(dist_sq)
            mask_pairs = pair_mask(own_cells, near_cells, shift_x, shift_y, True)
            rho_own = own_cells[4][..., :, None]
            reach_own = own_cells[5][..., :, None]
            rho_near = near_cells[4][..., None, :]
            reach_near = near_cells[5][..., None, :]
            denom_own = dist_sq + reach_near * reach_near + rho_own * rho_own
            denom_near = dist_sq + reach_own * reach_own + rho_near * rho_near
            slope_own = reach_near ** 3 * (taper_slope / denom_own ** 2 - 2.0 * taper_val / denom_own ** 3)
            slope_near = reach_own ** 3 * (taper_slope / denom_near ** 2 - 2.0 * taper_val / denom_near ** 3)
            gauss_fall = jnp.exp(-dist_sq / GAUSS_WIDTH_SQ)
            inner_prod = pair_inner(grad_message, near_feat) + pair_inner(own_feat, near_gmsg)
            pair_rate = mask_pairs * (grad_descreen[..., :, None] * slope_own + near_gdesc * slope_near + gauss_fall * (taper_slope - taper_val / GAUSS_WIDTH_SQ) * inner_prod)
            indirect = indirect + 2.0 * pair_push(pair_rate, own_cells, near_cells)
            grad_reach = grad_reach + lax.optimization_barrier(jnp.sum(mask_pairs * near_gdesc * taper_val * reach_own * reach_own * (3.0 / denom_near ** 2 - 4.0 * reach_own * reach_own / denom_near ** 3), axis=-1))
    return (indirect, grad_reach)

def pad_cells(array):
    return jnp.pad(array, ((0, 0), (1, 1), (1, 1), (0, 0)))

def pad_wide(array):
    return jnp.pad(array, ((1, 1), (1, 1), (0, 0), (0, 0)))

def block_slices(own_all, ext_all, row_start):
    own_cells = lax.dynamic_slice_in_dim(own_all, row_start, DEVICE_COLUMNS_X, axis=1)
    ext_cells = lax.dynamic_slice_in_dim(ext_all, row_start, DEVICE_COLUMNS_X + 2, axis=1)
    return (own_cells, ext_cells)

def wide_slices(own_all, ext_all, row_start):
    own_cells = lax.dynamic_slice_in_dim(own_all, row_start, DEVICE_COLUMNS_X, axis=0)
    ext_cells = lax.dynamic_slice_in_dim(ext_all, row_start, DEVICE_COLUMNS_X + 2, axis=0)
    return (own_cells, ext_cells)

def join_rows(stacked):
    return stacked.reshape((-1,) + stacked.shape[2:])

def join_blocks(stacked):
    moved = jnp.moveaxis(stacked, 0, 1)
    return moved.reshape((moved.shape[0], moved.shape[1] * moved.shape[2]) + moved.shape[3:])

def reference(positions, charges, slot_bead_types, cell_counts, features, radius_table, scale_table, mix_weight, out_weight, targets):
    total_slot_count = GRID_COLUMNS_X * GRID_COLUMNS_Y * COLUMN_SLOTS
    begin_offsets = jnp.arange(GRID_COLUMNS_X // DEVICE_COLUMNS_X, dtype=jnp.int32) * DEVICE_COLUMNS_X
    kind_range = jnp.arange(BEAD_KINDS, dtype=jnp.int32)
    force_list, energy_list, mix_list, out_list, scale_list = ([], [], [], [], [])
    for frame_idx in range(FRAME_COUNT):
        kind_hot = (slot_bead_types[frame_idx][None] == kind_range[:, None, None, None]).astype(jnp.float32)
        rho_all = lax.optimization_barrier(jnp.sum(kind_hot * radius_table[:, None, None, None], axis=0))
        reach_all = rho_all * lax.optimization_barrier(jnp.sum(kind_hot * scale_table[:, None, None, None], axis=0))
        valid_slot = (jnp.arange(COLUMN_SLOTS, dtype=jnp.int32)[None, None, :] < cell_counts[frame_idx][:, :, None]).astype(jnp.float32)
        own_all = jnp.concatenate([positions[:, frame_idx], charges[frame_idx][None], rho_all[None], reach_all[None], valid_slot[None]], axis=0)
        ext_all = pad_cells(own_all)
        feat_all = features[frame_idx]
        ext_feat = pad_wide(feat_all)

        def first_block(row_start):
            own_cells, ext_cells = block_slices(own_all, ext_all, row_start)
            feat_block, feat_ext = wide_slices(feat_all, ext_feat, row_start)
            return first_pass(own_cells, ext_cells, feat_block, feat_ext)
        descreen, messages = lax.map(first_block, begin_offsets)
        descreen = join_rows(descreen)
        message_low = join_rows(messages).astype(jnp.bfloat16)
        born_radius, hidden_act, tanh_screen, tanh_corr = born_radii(own_all, descreen, message_low, mix_weight, out_weight)
        born_all = born_radius[None]
        ext_born = pad_cells(born_all)

        def second_block(row_start):
            own_cells, ext_cells = block_slices(own_all, ext_all, row_start)
            born_block, born_ext = block_slices(born_all, ext_born, row_start)
            return second_pass(own_cells, ext_cells, born_block[0], born_ext)
        energy_blocks, grad_born, direct_grad = lax.map(second_block, begin_offsets)
        grad_born = join_rows(grad_born)
        direct_grad = join_blocks(direct_grad)
        grad_descreen, grad_corr = radius_backs(own_all, grad_born, tanh_screen, tanh_corr)
        grad_hidden = (grad_corr[..., None] * out_weight * (1.0 - hidden_act * hidden_act)).astype(jnp.bfloat16)
        grad_message = back_project(grad_hidden, mix_weight).astype(jnp.bfloat16)
        gdesc_all = grad_descreen[None]
        ext_gdesc = pad_cells(gdesc_all)
        ext_gmsg = pad_wide(grad_message)

        def third_block(row_start):
            own_cells, ext_cells = block_slices(own_all, ext_all, row_start)
            gdesc_block, gdesc_ext = block_slices(gdesc_all, ext_gdesc, row_start)
            gmsg_block, gmsg_ext = wide_slices(grad_message, ext_gmsg, row_start)
            feat_block, feat_ext = wide_slices(feat_all, ext_feat, row_start)
            return third_pass(own_cells, ext_cells, gdesc_block[0], gdesc_ext, gmsg_block, gmsg_ext, feat_block, feat_ext)
        indirect, grad_reach = lax.map(third_block, begin_offsets)
        indirect = join_blocks(indirect)
        grad_reach = join_rows(grad_reach)
        force_list.append(-(direct_grad + indirect))
        mix_part, out_part, scale_part = parameter_terms(own_all, kind_hot, grad_reach, message_low, grad_hidden, grad_corr, hidden_act)
        energy_list.append(jnp.sum(energy_blocks))
        mix_list.append(mix_part)
        out_list.append(out_part)
        scale_list.append(scale_part)
    energies = jnp.stack(energy_list) / total_slot_count
    weight = (energies - targets) / math.sqrt(total_slot_count)
    grad_mix = lax.optimization_barrier(jnp.sum(weight[:, None, None] * jnp.stack(mix_list), axis=0))
    grad_out = lax.optimization_barrier(jnp.sum(weight[:, None] * jnp.stack(out_list), axis=0))
    grad_scale = lax.optimization_barrier(jnp.sum(weight[:, None] * jnp.stack(scale_list), axis=0))
    forces = jnp.stack(force_list, axis=1)
    return (energies, forces, grad_mix, grad_out, grad_scale)
```

```python
import math

import jax
import jax.numpy as jnp
from jax import lax
from jax.experimental import pallas as pl
from jax.experimental.pallas import tpu as pltpu
from jax.sharding import PartitionSpec as P

SOLVENT = -0.5 * 0.98726
SCREEN_GAIN = 12.0
FAR = 4096.0
SLOTS = 128
ROWS = 160
CHUNK = 32
F32 = jnp.float32
BF16 = jnp.bfloat16


def split3(row):
    high = row.astype(BF16).astype(F32)
    rest = row - high
    mid = rest.astype(BF16).astype(F32)
    return [high, mid, rest - mid]


def pack_kernel(
    counts, radius, scale, pos_any, charge_any, kind_any, feat_any, mix_any, outw_any,
    low, high, mix_out, outw_out, pos, charge, kind, feat, sem,
):
    copies = [
        pltpu.make_async_copy(src, dst, sem.at[i])
        for i, (src, dst) in enumerate(
            (
                (pos_any, pos),
                (charge_any, charge),
                (kind_any, kind),
                (feat_any, feat),
                (mix_any, mix_out),
                (outw_any, outw_out),
            )
        )
    ]
    for copy in copies:
        copy.start()
    for copy in copies:
        copy.wait()
    slot = lax.broadcasted_iota(jnp.int32, (1, SLOTS), 1)
    zero = jnp.zeros((1, SLOTS), F32)
    kinds = jnp.concatenate(
        [kind[f, x, pl.ds(y, 1), :] for f in range(2) for x in range(2) for y in range(2)], axis=0
    )
    rho = jnp.zeros((8, SLOTS), F32)
    factor = jnp.zeros((8, SLOTS), F32)
    for k in range(32):
        rho = jnp.where(kinds == k, radius[k], rho)
        factor = jnp.where(kinds == k, scale[k], factor)
    reach = rho * factor
    for f in range(2):
        for x in range(2):
            for y in range(2):
                out = (low, high)[x]
                o = f * 4 + x * 2 + y
                rows = []
                for d in range(3):
                    rows += split3(pos[d, f, x, pl.ds(y, 1), :])
                rows += split3(charge[f, x, pl.ds(y, 1), :])
                rows += split3(rho[o : o + 1])
                rows += split3(reach[o : o + 1])
                rows.append(kinds[o : o + 1].astype(F32))
                rows.append((slot < counts[f, x, y]).astype(F32))
                rows += [zero] * (32 - len(rows))
                out[f, y, 0:SLOTS, :] = feat[f, x, y]
                out[f, y, SLOTS:ROWS, :] = jnp.concatenate(rows, axis=0).astype(BF16)


def chooser():
    r = lax.broadcasted_iota(jnp.int32, (16, 32), 0)
    k = lax.broadcasted_iota(jnp.int32, (16, 32), 1)
    triple = (r < 6) & (k >= 3 * r) & (k < 3 * r + 3)
    single = ((r == 6) | (r == 7)) & (k == r + 12)
    return jnp.where(triple | single, 1.0, 0.0).astype(BF16)


def decode(pick, coded):
    return jnp.dot(pick, coded, preferred_element_type=F32)


def near_rows(got):
    valid = got[7:8] > 0.0
    reach = got[5:6]
    square = reach * reach
    return [
        jnp.where(valid, got[0:1], -FAR),
        got[1:2],
        got[2:3],
        got[3:4],
        square,
        square * reach,
        got[4:5],
        got[6:7],
        got[7:8],
        jnp.where(valid, got[0:1], FAR),
        got[4:5] * got[4:5],
    ]


NX, NY, NZ, NQ, NR2, NR3, NRHO, NKIND, NVALID, OX, ORHO2 = range(11)


def spread_columns(rows, out):
    pad = [jnp.zeros((1, SLOTS), F32)] * (8 - len(rows))
    cols = jnp.transpose(jnp.concatenate(rows + pad, axis=0))
    for q in range(len(rows)):
        out[q] = jnp.broadcast_to(cols[:, q : q + 1], (SLOTS, SLOTS))


def self_far(start, size):
    r = lax.broadcasted_iota(jnp.int32, (size, SLOTS), 0) + start
    c = lax.broadcasted_iota(jnp.int32, (size, SLOTS), 1)
    return jnp.where(r == c, FAR * FAR, 0.0)


def keep_sum(pair, q, start, value):
    size = value.shape[0]
    high = value.astype(BF16)
    pair[q, 0, pl.ds(start, size), :] = high
    pair[q, 1, pl.ds(start, size), :] = (value - high.astype(F32)).astype(BF16)


def row_sum(pair, q):
    ones = jnp.ones((8, SLOTS), BF16)
    dims = (((1,), (1,)), ((), ()))
    high = lax.dot_general(ones, pair[q, 0], dims, preferred_element_type=F32)
    low = lax.dot_general(ones, pair[q, 1], dims, preferred_element_type=F32)
    return (high + low)[0:1]


def own_cell(o):
    return (o // 4) * 16 + ((o // 2) % 2 + 1) * 4 + o % 2 + 1


def halo_cells(o):
    base = (o // 4) * 16
    ox = (o // 2) % 2
    oy = o % 2
    across = [base + 12 * ox + oy + n for n in range(3)]
    return across + [base + 4 + 3 * oy, base + 8 + 3 * oy]


def gather_rows(ref, q, count=8):
    return jnp.concatenate([ref[o, q : q + 1, :] for o in range(count)], axis=0)


def unpack(pick, coded, c, dec, hot):
    rows = near_rows(decode(pick, coded))
    for q, row in enumerate(rows):
        dec[c, q : q + 1, :] = row
    kinds = lax.broadcasted_iota(jnp.int32, (32, SLOTS), 0).astype(F32)
    hot[c] = jnp.where(kinds == rows[NKIND], 1.0, 0.0).astype(BF16)


def first_blocks(cells, with_self, dec, feat, hot, colb, wgt, scl, pair, message, parts):
    size = CHUNK
    for r in range(0, SLOTS, size):
        sl = pl.ds(r, size)
        xi, yi, zi, ri2 = (colb[q, sl, :] for q in range(4))
        acc = None
        for n, c in enumerate(cells):
            rj2 = dec[c, NR2 : NR2 + 1, :]
            dx = xi - dec[c, NX : NX + 1, :]
            dy = yi - dec[c, NY : NY + 1, :]
            dz = zi - dec[c, NZ : NZ + 1, :]
            s = dx * dx + dy * dy + dz * dz
            if with_self and n == 0:
                s = s + self_far(r, size)
            m = jnp.maximum(1.0 - s, 0.0)
            t = m * m
            inv = 1.0 / (s + rj2 + ri2)
            ti = t * (inv * inv)
            term = ti * dec[c, NR3 : NR3 + 1, :]
            acc = term if acc is None else acc + term
            wgt[n, sl, :] = (t * jnp.exp(-4.0 * s)).astype(BF16)
            scl[n, sl, :] = (ti * (3.0 - (4.0 * rj2) * inv)).astype(BF16)
        keep_sum(pair, 0, r, acc)
    for n, c in enumerate(cells):
        message = message + jnp.dot(wgt[n], feat[c], preferred_element_type=F32)
        parts = parts + lax.dot_general(
            hot[c], scl[n], (((1,), (1,)), ((), ())), preferred_element_type=F32
        )
    return message, parts


def first_own_kernel(f, low, high, msg_out, part_out, scr_out, dec, feat, hot, colb, wgt, scl, pair):
    pick = chooser()
    for x in range(2):
        for y in range(2):
            o = x * 2 + y
            src = (low, high)[x]
            feat[o] = src[f, y, 0:SLOTS, :]
            unpack(pick, src[f, y, SLOTS:ROWS, :], o, dec, hot)

    def own(o, carry):
        spread_columns([dec[o, q : q + 1, :] for q in (OX, NY, NZ, ORHO2)], colb)
        cells = [o, o ^ 1, o ^ 2, o ^ 3]
        zero = jnp.zeros((SLOTS, SLOTS), F32)
        message, parts = first_blocks(
            cells, True, dec, feat, hot, colb, wgt, scl, pair, zero, zero[0:32]
        )
        msg_out[o] = message
        part_out[o] = parts
        scr_out[o] = jnp.broadcast_to(row_sum(pair, 0), (8, SLOTS))
        return carry

    lax.fori_loop(0, 4, own, 0)


def first_halo_kernel(
    low, high, xlow, xhigh, ylow, yhigh, msg0, msg1, part0, part1, scr0, scr1, mix, outw,
    dec, feat, bead, act_out, msg_out, part_out, hot, colb, wgt, scl, pair, sums,
):
    pick = chooser()
    for f in range(2):
        for ex in range(4):
            for ey in range(4):
                c = f * 16 + ex * 4 + ey
                if ey == 0:
                    src, a = ylow, ex
                elif ey == 3:
                    src, a = yhigh, ex
                else:
                    src, a = (xlow, low, high, xhigh)[ex], ey - 1
                feat[c] = src[f, a, 0:SLOTS, :]
                unpack(pick, src[f, a, SLOTS:ROWS, :], c, dec, hot)
    weight = outw[...]

    for f, (msg_in, part_in, scr_in) in enumerate(((msg0, part0, scr0), (msg1, part1, scr1))):

        def own(k, carry, f=f, msg_in=msg_in, part_in=part_in, scr_in=scr_in):
            o = 4 * f + k
            me = own_cell(o)
            spread_columns([dec[me, q : q + 1, :] for q in (OX, NY, NZ, ORHO2)], colb)
            message, parts = first_blocks(
                halo_cells(o), False, dec, feat, hot, colb, wgt, scl, pair, msg_in[k], part_in[k]
            )
            part_out[o] = parts
            message = message.astype(BF16)
            msg_out[o] = message
            act = jnp.tanh(jnp.dot(message, mix[...], preferred_element_type=F32))
            act_out[o] = act
            keep_sum(pair, 1, 0, act * weight)
            sums[o, 0:1, :] = row_sum(pair, 0) + scr_in[k, 0:1, :]
            sums[o, 1:2, :] = row_sum(pair, 1)
            return carry

        lax.fori_loop(0, 4, own, 0)
    cells = [own_cell(o) for o in range(8)]
    rho = jnp.concatenate([dec[c, NRHO : NRHO + 1, :] for c in cells], axis=0)
    valid = jnp.concatenate([dec[c, NVALID : NVALID + 1, :] for c in cells], axis=0)
    tanh_screen = jnp.tanh(SCREEN_GAIN * rho * gather_rows(sums, 0))
    tanh_corr = jnp.tanh(gather_rows(sums, 1))
    born = rho * (1.0 + 0.5 * tanh_corr) / (1.0 - 0.8 * tanh_screen)
    bead[0] = jnp.where(valid > 0.0, born, 1.0)
    bead[1] = tanh_screen
    bead[2] = tanh_corr
    bead[3] = rho


def second_blocks(cells, seats, with_self, dec, born, colb, pair):
    size = CHUNK // 2
    for r in range(0, SLOTS, size):
        sl = pl.ds(r, size)
        xi, yi, zi, bi, ibi = (colb[q, sl, :] for q in range(5))
        acc = None
        for n, (c, b) in enumerate(zip(cells, seats)):
            bj = born[b, 0:1, :]
            dx = xi - dec[c, NX : NX + 1, :]
            dy = yi - dec[c, NY : NY + 1, :]
            dz = zi - dec[c, NZ : NZ + 1, :]
            s = dx * dx + dy * dy + dz * dz
            if with_self and n == 0:
                s = s + self_far(r, size)
            m = jnp.maximum(1.0 - s, 0.0)
            arg = s * (ibi * born[b, 1:2, :])
            g = jnp.exp(-arg)
            rinv = lax.rsqrt(s + bi * bj * g)
            isq = rinv * rinv
            mq = m * dec[c, NQ : NQ + 1, :] * rinv
            et = m * mq
            rate = mq * (2.0 + (0.5 * m) * (1.0 - 0.25 * g) * isq)
            terms = [et, et * isq * (g * (1.0 + arg)) * bj, rate * dx, rate * dy, rate * dz]
            acc = terms if acc is None else [a + t for a, t in zip(acc, terms)]
        for q in range(5):
            keep_sum(pair, q, r, acc[q])


def second_own_kernel(f, dec, bead, part, colb, pair, born):
    for k in range(4):
        o = 4 * f + k
        born[k, 0:1, :] = bead[0, o : o + 1, :]
        born[k, 1:2, :] = 1.0 / bead[0, o : o + 1, :]

    def own(k, carry):
        me = own_cell(k + 4 * f)
        spread_columns(
            [dec[me, q : q + 1, :] for q in (OX, NY, NZ)]
            + [born[k, 0:1, :], 0.25 * born[k, 1:2, :]],
            colb,
        )
        seats = [k, k ^ 1, k ^ 2, k ^ 3]
        second_blocks([own_cell(b + 4 * f) for b in seats], seats, True, dec, born, colb, pair)
        for q in range(5):
            part[k, q : q + 1, :] = row_sum(pair, q)
        return carry

    lax.fori_loop(0, 4, own, 0)


def second_halo_kernel(
    dec, bead, xlow, xhigh, ylow, yhigh, part0, part1, act, message, parts, mix, outw,
    grad_psi, grad_message, direct, mix_out, tail_out, colb, pair, born, sums,
):
    for f in range(2):
        for ex in range(4):
            for ey in range(4):
                c = f * 16 + ex * 4 + ey
                if ey == 0:
                    row = ylow[f, pl.ds(ex, 1), :]
                elif ey == 3:
                    row = yhigh[f, pl.ds(ex, 1), :]
                elif ex == 0:
                    row = xlow[f, pl.ds(ey - 1, 1), :]
                elif ex == 3:
                    row = xhigh[f, pl.ds(ey - 1, 1), :]
                else:
                    o = f * 4 + (ex - 1) * 2 + ey - 1
                    row = bead[0, o : o + 1, :]
                row = jnp.where(dec[c, NVALID : NVALID + 1, :] > 0.0, row, 1.0)
                born[c, 0:1, :] = row
                born[c, 1:2, :] = 1.0 / row

    def own(o, carry):
        me = own_cell(o)
        spread_columns(
            [dec[me, q : q + 1, :] for q in (OX, NY, NZ)]
            + [born[me, 0:1, :], 0.25 * born[me, 1:2, :]],
            colb,
        )
        cells = halo_cells(o)
        second_blocks(cells, cells, False, dec, born, colb, pair)
        for q in range(5):
            sums[o, q : q + 1, :] = row_sum(pair, q)
        return carry

    lax.fori_loop(0, 8, own, 0)
    for q in range(5):
        for k in range(4):
            sums[k, q : q + 1, :] += part0[k, q : q + 1, :]
            sums[k + 4, q : q + 1, :] += part1[k, q : q + 1, :]
    total = [gather_rows(sums, q) for q in range(5)]
    cells = [own_cell(o) for o in range(8)]
    charge = jnp.concatenate([dec[c, NQ : NQ + 1, :] for c in cells], axis=0)
    valid = jnp.concatenate([dec[c, NVALID : NVALID + 1, :] for c in cells], axis=0)
    inv = 1.0 / bead[0]
    scaled = SOLVENT * charge
    self_energy = scaled * charge * valid * inv
    energy = scaled * total[0] + self_energy
    grad_born = -scaled * total[1] - self_energy * inv
    for d in range(3):
        direct[d] = -4.0 * scaled * total[2 + d]
    tanh_screen, tanh_corr, rho = bead[1], bead[2], bead[3]
    down = 1.0 - 0.8 * tanh_screen
    psi = (
        SCREEN_GAIN * rho * grad_born * rho * (1.0 + 0.5 * tanh_corr) * 0.8
        * (1.0 - tanh_screen * tanh_screen) / (down * down)
    )
    grad_psi[...] = psi
    grad_corr = grad_born * rho * 0.5 * (1.0 - tanh_corr * tanh_corr) / down
    corr_cols = jnp.transpose(grad_corr)
    weight = outw[...]
    kind = lax.broadcasted_iota(jnp.int32, (32, SLOTS), 0)
    lane = lax.broadcasted_iota(jnp.int32, (32, SLOTS), 1)
    for f in range(2):
        mix_sum = None
        for k in range(4):
            o = f * 4 + k
            col = corr_cols[:, o : o + 1]
            hidden = act[o]
            grad_hidden = (col * weight * (1.0 - hidden * hidden)).astype(BF16)
            grad_message[o] = lax.dot_general(
                grad_hidden, mix[...], (((1,), (1,)), ((), ())), preferred_element_type=F32
            ).astype(BF16)
            term = lax.dot_general(
                message[o], grad_hidden, (((0,), (0,)), ((), ())), preferred_element_type=F32
            )
            out_term = jnp.sum(col * hidden, axis=0, keepdims=True)
            scale_term = psi[o : o + 1] * parts[o]
            if mix_sum is None:
                mix_sum, out_sum, scale_sum = term, out_term, scale_term
            else:
                mix_sum = mix_sum + term
                out_sum = out_sum + out_term
                scale_sum = scale_sum + scale_term
        mix_out[f] = mix_sum
        both = jnp.sum(energy[f * 4 : f * 4 + 4], axis=0, keepdims=True)
        both = jnp.sum(both, axis=1, keepdims=True)
        scale_col = jnp.sum(scale_sum, axis=1, keepdims=True)
        scale_row = jnp.sum(jnp.where(kind == lane, scale_col, 0.0), axis=0, keepdims=True)
        tail_out[f] = jnp.concatenate(
            [out_sum, jnp.broadcast_to(both, (1, SLOTS)), scale_row, jnp.zeros((5, SLOTS), F32)],
            axis=0,
        )


def fold8(value):
    total = value[0:8]
    for r in range(8, value.shape[0], 8):
        total = total + value[r : r + 8]
    return total


def third_kernel(first, count, dec, feat, grad_psi, grad_message, out, colb, pair, jacc, inner):
    for k in range(count):
        o = first + k
        me = own_cell(o)
        cells = [me - 5 + (n // 3) * 4 + n % 3 for n in range(9)]
        spread_columns(
            [dec[me, q : q + 1, :] for q in (OX, NY, NZ, ORHO2)] + [grad_psi[o : o + 1, :]], colb
        )
        gmsg = grad_message[o]
        for n, c in enumerate(cells):
            inner[n] = lax.dot_general(
                gmsg, feat[c], (((1,), (1,)), ((), ())), preferred_element_type=F32
            )
        for r in range(0, SLOTS, CHUNK):
            sl = pl.ds(r, CHUNK)
            xi, yi, zi, ri2, gp = (colb[q, sl, :] for q in range(5))
            acc = None
            for n, c in enumerate(cells):
                dx = xi - dec[c, NX : NX + 1, :]
                dy = yi - dec[c, NY : NY + 1, :]
                dz = zi - dec[c, NZ : NZ + 1, :]
                s = dx * dx + dy * dy + dz * dz
                if n == 4:
                    s = s + self_far(r, CHUNK)
                m = jnp.maximum(1.0 - s, 0.0)
                inv = 1.0 / (s + dec[c, NR2 : NR2 + 1, :] + ri2)
                slope = dec[c, NR3 : NR3 + 1, :] * (inv * inv) * gp * (1.0 + m * inv)
                gauss = jnp.exp(-4.0 * s) * (1.0 + 2.0 * m) * inner[n, sl, :]
                rate = m * (slope + gauss)
                terms = [rate * dx, rate * dy, rate * dz]
                acc = terms if acc is None else [a + t for a, t in zip(acc, terms)]
                for d in range(3):
                    folded = fold8(terms[d])
                    if r == 0:
                        jacc[n, d] = folded
                    else:
                        jacc[n, d] += folded
            for d in range(3):
                keep_sum(pair, d, r, acc[d])
        for d in range(3):
            for n in range(9):
                out[k, d, n : n + 1, :] = jnp.sum(jacc[n, d], axis=0, keepdims=True)
            out[k, d, 9:10, :] = row_sum(pair, d)
            out[k, d, 10:16, :] = jnp.zeros((6, SLOTS), F32)


def gather_kernel(count, *refs):
    pieces, direct, ext = refs[: 8 // count], refs[-2], refs[-1]
    for f in range(2):
        for ex in range(4):
            for ey in range(4):
                for d in range(3):
                    value = None
                    for k in range(4):
                        n = (ex - k // 2, ey - k % 2)
                        if not (0 <= n[0] < 3 and 0 <= n[1] < 3):
                            continue
                        o = f * 4 + k
                        piece = pieces[o // count]
                        row = n[0] * 3 + n[1]
                        term = piece[o % count, d, row : row + 1, :]
                        value = term if value is None else value + term
                    value = -4.0 * value
                    if ex in (1, 2) and ey in (1, 2):
                        o = f * 4 + (ex - 1) * 2 + ey - 1
                        piece = pieces[o // count]
                        value = value - direct[d, o : o + 1, :]
                        value = value + 4.0 * piece[o % count, d, 9:10, :]
                    ext[d, f, ex, pl.ds(ey, 1), :] = value


def weigh_kernel(slots, core, targets, sums, out):
    row = sums[SLOTS + 1 : SLOTS + 2, :]
    target = jnp.where(core[0] == 0, targets[0], targets[1])
    weight = (row * (1.0 / slots) - target) * (1.0 / math.sqrt(slots))
    out[...] = sums[...] * weight
    out[SLOTS + 1 : SLOTS + 2, :] = row


def vmem(count):
    return [pl.BlockSpec(memory_space=pltpu.VMEM)] * count


def smem(count):
    return [pl.BlockSpec(memory_space=pltpu.SMEM)] * count


def shape(*dims, dtype=F32):
    return jax.ShapeDtypeStruct(dims, dtype)


def square(*lead, dtype=F32):
    return pltpu.VMEM(lead + (SLOTS, SLOTS), dtype)


def call(kernel, name, in_specs, out_shape, scratch, flops=1000000):
    single = not isinstance(out_shape, tuple)
    return pl.pallas_call(
        kernel,
        name=name,
        in_specs=in_specs,
        out_specs=vmem(1)[0] if single else tuple(vmem(len(out_shape))),
        out_shape=out_shape,
        scratch_shapes=scratch,
        compiler_params=pltpu.CompilerParams(vmem_limit_bytes=40 << 20),
        cost_estimate=pl.CostEstimate(flops=flops, transcendentals=0, bytes_accessed=1 << 20),
    )


def chain(axis):
    count = lax.axis_size(axis)
    forward = [(i, i + 1) for i in range(count - 1)]
    return forward, [(b, a) for a, b in forward]


def exchange(low, high, axis):
    forward, backward = chain(axis)
    return lax.ppermute(high, axis, forward), lax.ppermute(low, axis, backward)


def flip(value, axis, bit):
    return lax.ppermute(value, axis, [(i, i ^ bit) for i in range(lax.axis_size(axis))])


PIECE = 2


def on_device(
    positions, charges, slot_bead_types, cell_counts, features,
    radius_table, scale_table, mix_weight, out_weight, targets,
):
    total_slots = 2 * lax.axis_size("gx") * 2 * lax.axis_size("gy") * SLOTS
    edge = shape(2, 2, ROWS, SLOTS, dtype=BF16)
    low, high, mix, outw = call(
        pack_kernel, "pack", smem(3) + [pl.BlockSpec(memory_space=pltpu.HBM)] * 6,
        (edge, edge, shape(SLOTS, SLOTS, dtype=BF16), shape(1, SLOTS)),
        [pltpu.VMEM((3, 2, 2, 2, SLOTS), F32), pltpu.VMEM((2, 2, 2, SLOTS), F32),
         pltpu.VMEM((2, 2, 2, SLOTS), jnp.int32), square(2, 2, 2, dtype=BF16),
         pltpu.SemaphoreType.DMA((6,))],
        10000,
    )(cell_counts, radius_table, scale_table, positions, charges, slot_bead_types, features,
      mix_weight, out_weight.reshape(1, SLOTS))

    def first_own(f, low, high):
        return call(
            lambda *refs: first_own_kernel(f, *refs), f"first_own{f}", vmem(2),
            (shape(4, SLOTS, SLOTS), shape(4, 32, SLOTS), shape(4, 8, SLOTS)),
            [pltpu.VMEM((4, 16, SLOTS), F32), square(4, dtype=BF16),
             pltpu.VMEM((4, 32, SLOTS), BF16), square(4), square(4, dtype=BF16),
             square(4, dtype=BF16), square(1, 2, dtype=BF16)],
        )(low, high)

    xlow, xhigh = exchange(low, high, "gx")
    half0 = first_own(0, low, high)
    xlow, xhigh, low, high, half0 = lax.optimization_barrier((xlow, xhigh, low, high, half0))
    bottom = jnp.stack([v[:, 0] for v in (xlow, low, high, xhigh)], axis=1)
    top = jnp.stack([v[:, 1] for v in (xlow, low, high, xhigh)], axis=1)
    ylow, yhigh = exchange(bottom, top, "gy")
    half1 = first_own(1, low, high)
    (msg0, part0, scr0), (msg1, part1, scr1) = half0, half1

    dec, feat, bead, act, message, parts = call(
        first_halo_kernel, "first_halo", vmem(14),
        (shape(32, 16, SLOTS), shape(32, SLOTS, SLOTS, dtype=BF16), shape(4, 8, SLOTS),
         shape(8, SLOTS, SLOTS), shape(8, SLOTS, SLOTS, dtype=BF16), shape(8, 32, SLOTS)),
        [pltpu.VMEM((32, 32, SLOTS), BF16), square(4), square(5, dtype=BF16),
         square(5, dtype=BF16), square(2, 2, dtype=BF16), pltpu.VMEM((8, 8, SLOTS), F32)],
    )(low, high, xlow, xhigh, ylow, yhigh, msg0, msg1, part0, part1, scr0, scr1, mix, outw)

    def second_own(f, dec, bead):
        return call(
            lambda *refs: second_own_kernel(f, *refs), f"second_own{f}", vmem(2),
            shape(4, 8, SLOTS),
            [square(5), square(5, 2, dtype=BF16), pltpu.VMEM((4, 8, SLOTS), F32)],
        )(dec, bead)

    born = bead[0].reshape(2, 2, 2, SLOTS)
    bxlow, bxhigh = exchange(born[:, 0], born[:, 1], "gx")
    sums0 = second_own(0, dec, bead)
    bxlow, bxhigh, bead, sums0 = lax.optimization_barrier((bxlow, bxhigh, bead, sums0))
    bottom = jnp.stack([bxlow[:, 0], born[:, 0, 0], born[:, 1, 0], bxhigh[:, 0]], axis=1)
    top = jnp.stack([bxlow[:, 1], born[:, 0, 1], born[:, 1, 1], bxhigh[:, 1]], axis=1)
    bylow, byhigh = exchange(bottom, top, "gy")
    sums1 = second_own(1, dec, bead)

    grad_psi, grad_message, direct, mix_part, tail = call(
        second_halo_kernel, "second_halo", vmem(13),
        (shape(8, SLOTS), shape(8, SLOTS, SLOTS, dtype=BF16), shape(3, 8, SLOTS),
         shape(2, SLOTS, SLOTS), shape(2, 8, SLOTS)),
        [square(5), square(5, 2, dtype=BF16), pltpu.VMEM((32, 8, SLOTS), F32),
         pltpu.VMEM((8, 8, SLOTS), F32)],
    )(dec, bead, bxlow, bxhigh, bylow, byhigh, sums0, sums1, act, message, parts, mix, outw)

    def third(first, grad_psi):
        return call(
            lambda *refs: third_kernel(first, PIECE, *refs), f"third{first}", vmem(4),
            shape(PIECE, 3, 16, SLOTS),
            [square(5), square(3, 2, dtype=BF16), pltpu.VMEM((9, 3, 8, SLOTS), F32), square(9)],
        )(dec, feat, grad_psi, grad_message)

    payload = jnp.concatenate([mix_part, tail], axis=1)
    core = lax.axis_index("gy") % 2
    sent = jnp.where(core == 0, payload[1], payload[0])
    kept = jnp.where(core == 0, payload[0], payload[1])
    steps = [("gy", 1)]
    for axis, first in (("gx", 1), ("gy", 2)):
        bit = first
        while bit < lax.axis_size(axis):
            steps.append((axis, bit))
            bit *= 2
    pieces = []
    sums = kept
    rows = forces = None
    for i, (axis, bit) in enumerate(steps):
        other = flip(sent if i == 0 else sums, axis, bit)
        if len(pieces) < 8 // PIECE:
            piece = third(PIECE * len(pieces), grad_psi)
            other, grad_psi, piece = lax.optimization_barrier((other, grad_psi, piece))
            pieces.append(piece)
            if len(pieces) == 8 // PIECE:
                ext = call(
                    lambda *refs: gather_kernel(PIECE, *refs), "gather", vmem(8 // PIECE + 1),
                    shape(3, 2, 4, 4, SLOTS), [],
                )(*pieces, direct)
        elif rows is None:
            forward, backward = chain("gy")
            from_high = lax.ppermute(ext[:, :, :, 0], "gy", backward)
            from_low = lax.ppermute(ext[:, :, :, 3], "gy", forward)
            rows = jnp.stack([ext[:, :, :, 1] + from_low, ext[:, :, :, 2] + from_high], axis=3)
        elif forces is None:
            forward, backward = chain("gx")
            from_high = lax.ppermute(rows[:, :, 0], "gx", backward)
            from_low = lax.ppermute(rows[:, :, 3], "gx", forward)
            forces = jnp.stack([rows[:, :, 1] + from_low, rows[:, :, 2] + from_high], axis=2)
        sums = sums + other

    scaled = call(
        lambda *refs: weigh_kernel(total_slots, *refs), "weigh", smem(2) + vmem(1),
        shape(SLOTS + 8, SLOTS), [], 1000,
    )(core.reshape(1).astype(jnp.int32), targets, sums)
    partner = flip(scaled, "gy", 1)
    joined = scaled + partner
    mine, theirs = scaled[SLOTS + 1, 0], partner[SLOTS + 1, 0]
    energies = jnp.where(core == 0, jnp.stack([mine, theirs]), jnp.stack([theirs, mine])) / total_slots
    reach = radius_table * scale_table
    factor = radius_table * reach * reach
    return (energies, forces, joined[:SLOTS], joined[SLOTS], joined[SLOTS + 2, :32] * factor)


def solution(mesh):
    placed = (
        P(None, None, "gx", "gy", None),
        P(None, "gx", "gy", None),
        P(None, "gx", "gy", None),
        P(None, "gx", "gy"),
        P(None, "gx", "gy", None, None),
        P(),
        P(),
        P(),
        P(),
        P(),
    )
    return jax.shard_map(
        on_device,
        mesh=mesh,
        in_specs=placed,
        out_specs=(P(), P(None, None, "gx", "gy", None), P(), P(), P()),
        check_vma=False,
    )
```

```python
import math

import jax
import jax.numpy as jnp
from jax import lax
from jax.experimental import pallas as pl
from jax.experimental.pallas import tpu as pltpu
from jax.sharding import PartitionSpec as P

SOLVENT = -0.5 * 0.98726
SCREEN_GAIN = 12.0
FAR = 4096.0
SLOTS = 128
ROWS = 160
CHUNK = 32
F32 = jnp.float32
BF16 = jnp.bfloat16


def split3(row):
    high = row.astype(BF16).astype(F32)
    rest = row - high
    mid = rest.astype(BF16).astype(F32)
    return [high, mid, rest - mid]


def pack_kernel(
    count_any, radius_any, scale_any, pos_any, charge_any, kind_any, feat_any, mix_any, outw_any,
    kept, sent, mix_out, outw_out, factor_out, counts, radius, scale, pos, charge, kind, feat, sem,
):
    copies = [
        pltpu.make_async_copy(src, dst, sem.at[i])
        for i, (src, dst) in enumerate(
            (
                (pos_any, pos),
                (charge_any, charge),
                (kind_any, kind),
                (feat_any, feat),
                (mix_any, mix_out),
                (outw_any, outw_out),
                (count_any, counts),
                (radius_any, radius),
                (scale_any, scale),
            )
        )
    ]
    for copy in copies:
        copy.start()
    for copy in copies:
        copy.wait()
    place = lax.axis_index("gy")
    core = place % 2
    upper = place // 2
    slot = lax.broadcasted_iota(jnp.int32, (1, SLOTS), 1)
    zero = jnp.zeros((1, SLOTS), F32)
    spots = [(s, x, y) for s in range(2) for x in range(2) for y in range(2)]

    def seat(s, y):
        frame = core if s == 0 else 1 - core
        row = upper if y == 0 else 1 - upper
        return frame, row

    found = []
    for s, x, y in spots:
        frame, row = seat(s, y)
        found.append(kind[frame, x, pl.ds(row, 1), :])
    kinds = jnp.concatenate(found, axis=0)
    rho = jnp.zeros((8, SLOTS), F32)
    factor = jnp.zeros((8, SLOTS), F32)
    for k in range(32):
        rho = jnp.where(kinds == k, radius[k], rho)
        factor = jnp.where(kinds == k, scale[k], factor)
    reach = rho * factor
    weights = jnp.zeros((1, SLOTS), F32)
    for k in range(32):
        span = radius[k] * scale[k]
        weights = jnp.where(slot == k, radius[k] * span * span, weights)
    factor_out[...] = weights
    for o, (s, x, y) in enumerate(spots):
        frame, row = seat(s, y)
        out = (kept, sent)[s]
        rows = []
        for d in range(3):
            rows += split3(pos[d, frame, x, pl.ds(row, 1), :])
        rows += split3(charge[frame, x, pl.ds(row, 1), :])
        rows += split3(rho[o : o + 1])
        rows += split3(reach[o : o + 1])
        rows.append(kinds[o : o + 1].astype(F32))
        rows.append((slot < counts[frame, x, row]).astype(F32))
        rows += [zero] * (32 - len(rows))
        out[x, y, 0:SLOTS, :] = feat[frame, x, row]
        out[x, y, SLOTS:ROWS, :] = jnp.concatenate(rows, axis=0).astype(BF16)


def chooser():
    r = lax.broadcasted_iota(jnp.int32, (16, 32), 0)
    k = lax.broadcasted_iota(jnp.int32, (16, 32), 1)
    triple = (r < 6) & (k >= 3 * r) & (k < 3 * r + 3)
    single = ((r == 6) | (r == 7)) & (k == r + 12)
    return jnp.where(triple | single, 1.0, 0.0).astype(BF16)


def decode(pick, coded):
    return jnp.dot(pick, coded, preferred_element_type=F32)


def near_rows(got):
    valid = got[7:8] > 0.0
    reach = got[5:6]
    square = reach * reach
    return [
        jnp.where(valid, got[0:1], -FAR),
        got[1:2],
        got[2:3],
        got[3:4],
        square,
        square * reach,
        got[4:5],
        got[6:7],
        got[7:8],
        jnp.where(valid, got[0:1], FAR),
        got[4:5] * got[4:5],
    ]


NX, NY, NZ, NQ, NR2, NR3, NRHO, NKIND, NVALID, OX, ORHO2 = range(11)


def spread_columns(rows, out):
    pad = [jnp.zeros((1, SLOTS), F32)] * (8 - len(rows))
    cols = jnp.transpose(jnp.concatenate(rows + pad, axis=0))
    for q in range(len(rows)):
        out[q] = jnp.broadcast_to(cols[:, q : q + 1], (SLOTS, SLOTS))


def self_far(start, size):
    r = lax.broadcasted_iota(jnp.int32, (size, SLOTS), 0) + start
    c = lax.broadcasted_iota(jnp.int32, (size, SLOTS), 1)
    return jnp.where(r == c, FAR * FAR, 0.0)


def keep_sum(pair, q, start, value):
    size = value.shape[0]
    high = value.astype(BF16)
    pair[q, 0, pl.ds(start, size), :] = high
    pair[q, 1, pl.ds(start, size), :] = (value - high.astype(F32)).astype(BF16)


def row_sum(pair, q):
    ones = jnp.ones((8, SLOTS), BF16)
    dims = (((1,), (1,)), ((), ()))
    high = lax.dot_general(ones, pair[q, 0], dims, preferred_element_type=F32)
    low = lax.dot_general(ones, pair[q, 1], dims, preferred_element_type=F32)
    return (high + low)[0:1]


def own_cell(o):
    return (o // 4 + 1) * 5 + o % 4


def near_own(o):
    x, v = o // 4, o % 4
    rows = [w for w in (v, v - 1, v + 1) if 0 <= w < 4]
    return [x * 4 + w for w in rows] + [(1 - x) * 4 + w for w in rows]


def near_halo(o):
    x, v = o // 4, o % 4
    cells = [15 * x + w for w in (v - 1, v, v + 1) if w >= 0]
    return cells + ([9, 14] if v == 3 else [])


def near_all(o):
    x, v = o // 4, o % 4
    spots = [(0, 0)] + [(p, q) for p in (-1, 0, 1) for q in (-1, 0, 1) if (p, q) != (0, 0)]
    return [(x + 1 + p, v + q) for p, q in spots if v + q >= 0]


def gather_rows(ref, q, count=8):
    return jnp.concatenate([ref[o, q : q + 1, :] for o in range(count)], axis=0)


def unpack(pick, coded, c, dec, hot):
    rows = near_rows(decode(pick, coded))
    for q, row in enumerate(rows):
        dec[c, q : q + 1, :] = row
    kinds = lax.broadcasted_iota(jnp.int32, (32, SLOTS), 0).astype(F32)
    hot[c] = jnp.where(kinds == rows[NKIND], 1.0, 0.0).astype(BF16)


def first_blocks(cells, with_self, dec, feat, hot, colb, wgt, scl, pair, message, parts):
    size = CHUNK
    for r in range(0, SLOTS, size):
        sl = pl.ds(r, size)
        xi, yi, zi, ri2 = (colb[q, sl, :] for q in range(4))
        acc = None
        for n, c in enumerate(cells):
            rj2 = dec[c, NR2 : NR2 + 1, :]
            dx = xi - dec[c, NX : NX + 1, :]
            dy = yi - dec[c, NY : NY + 1, :]
            dz = zi - dec[c, NZ : NZ + 1, :]
            s = dx * dx + dy * dy + dz * dz
            if with_self and n == 0:
                s = s + self_far(r, size)
            m = jnp.maximum(1.0 - s, 0.0)
            t = m * m
            inv = 1.0 / (s + rj2 + ri2)
            ti = t * (inv * inv)
            term = ti * dec[c, NR3 : NR3 + 1, :]
            acc = term if acc is None else acc + term
            wgt[n, sl, :] = (t * jnp.exp(-4.0 * s)).astype(BF16)
            scl[n, sl, :] = (ti * (3.0 - (4.0 * rj2) * inv)).astype(BF16)
        keep_sum(pair, 0, r, acc)
    for n, c in enumerate(cells):
        term = jnp.dot(wgt[n], feat(c), preferred_element_type=F32)
        part = lax.dot_general(
            hot[c], scl[n], (((1,), (1,)), ((), ())), preferred_element_type=F32
        )
        message = term if message is None else message + term
        parts = part if parts is None else parts + part
    return message, parts


def first_own_kernel(low, high, msg_out, part_out, scr_out, dec, hot, colb, wgt, scl, pair):
    pick = chooser()
    for x in range(2):
        for v in range(4):
            unpack(pick, (low, high)[x][v, SLOTS:ROWS, :], x * 4 + v, dec, hot)
    for o in range(8):
        spread_columns([dec[o, q : q + 1, :] for q in (OX, NY, NZ, ORHO2)], colb)
        message, parts = first_blocks(
            near_own(o), True, dec, lambda c: (low, high)[c // 4][c % 4, 0:SLOTS, :],
            hot, colb, wgt, scl, pair, None, None,
        )
        msg_out[o] = message
        part_out[o] = parts
        scr_out[o] = jnp.broadcast_to(row_sum(pair, 0), (8, SLOTS))


def cell_source(refs, c):
    ex, v = c // 5, c % 5
    return refs[4].at[ex] if v == 4 else refs[ex].at[v]


def first_side_kernel(
    xlow, low, high, xhigh, msg_in, part_in, scr_in,
    dec, hot, msg_out, part_out, scr_out, colb, wgt, scl, pair,
):
    pick = chooser()
    refs = (xlow, low, high, xhigh)
    for ex in range(4):
        for v in range(4):
            unpack(pick, refs[ex][v, SLOTS:ROWS, :], ex * 5 + v, dec, hot)
        dec[ex * 5 + 4] = jnp.zeros((16, SLOTS), F32)
        hot[ex * 5 + 4] = jnp.zeros((32, SLOTS), BF16)
    for o in range(8):
        me = own_cell(o)
        spread_columns([dec[me, q : q + 1, :] for q in (OX, NY, NZ, ORHO2)], colb)
        message, parts = first_blocks(
            [c for c in near_halo(o) if c % 5 != 4], False, dec,
            lambda c: refs[c // 5][c % 5, 0:SLOTS, :],
            hot, colb, wgt, scl, pair, msg_in[o], part_in[o],
        )
        msg_out[o] = message
        part_out[o] = parts
        scr_out[o] = scr_in[o] + row_sum(pair, 0)


def first_halo_kernel(
    dec_in, hot_in, yrow, msg_in, part_in, scr_in, mix, outw,
    dec, bead, act_out, msg_out, part_out, hot, colb, wgt, scl, pair, sums,
):
    pick = chooser()
    dec[...] = dec_in[...]
    hot[...] = hot_in[...]
    for ex in range(4):
        unpack(pick, yrow[ex, SLOTS:ROWS, :], ex * 5 + 4, dec, hot)
    weight = outw[...]
    for o in range(8):
        me = own_cell(o)
        message, parts = msg_in[o], part_in[o]
        screen = scr_in[o, 0:1, :]
        if o % 4 == 3:
            spread_columns([dec[me, q : q + 1, :] for q in (OX, NY, NZ, ORHO2)], colb)
            message, parts = first_blocks(
                [c for c in near_halo(o) if c % 5 == 4], False, dec,
                lambda c: yrow[c // 5, 0:SLOTS, :],
                hot, colb, wgt, scl, pair, message, parts,
            )
            screen = screen + row_sum(pair, 0)
        part_out[o] = parts
        message = message.astype(BF16)
        msg_out[o] = message
        act = jnp.tanh(jnp.dot(message, mix[...], preferred_element_type=F32))
        act_out[o] = act
        keep_sum(pair, 1, 0, act * weight)
        sums[o, 0:1, :] = screen
        sums[o, 1:2, :] = row_sum(pair, 1)
    cells = [own_cell(o) for o in range(8)]
    rho = jnp.concatenate([dec[c, NRHO : NRHO + 1, :] for c in cells], axis=0)
    valid = jnp.concatenate([dec[c, NVALID : NVALID + 1, :] for c in cells], axis=0)
    tanh_screen = jnp.tanh(SCREEN_GAIN * rho * gather_rows(sums, 0))
    tanh_corr = jnp.tanh(gather_rows(sums, 1))
    born = rho * (1.0 + 0.5 * tanh_corr) / (1.0 - 0.8 * tanh_screen)
    bead[0] = jnp.where(valid > 0.0, born, 1.0)
    bead[1] = tanh_screen
    bead[2] = tanh_corr
    bead[3] = rho


def second_blocks(cells, with_self, dec, born, colb, pair):
    size = CHUNK // 2
    for r in range(0, SLOTS, size):
        sl = pl.ds(r, size)
        xi, yi, zi, bi, ibi = (colb[q, sl, :] for q in range(5))
        acc = None
        for n, c in enumerate(cells):
            bj = born[c, 0:1, :]
            dx = xi - dec[c, NX : NX + 1, :]
            dy = yi - dec[c, NY : NY + 1, :]
            dz = zi - dec[c, NZ : NZ + 1, :]
            s = dx * dx + dy * dy + dz * dz
            if with_self and n == 0:
                s = s + self_far(r, size)
            m = jnp.maximum(1.0 - s, 0.0)
            arg = s * (ibi * born[c, 1:2, :])
            g = jnp.exp(-arg)
            rinv = lax.rsqrt(s + bi * bj * g)
            isq = rinv * rinv
            mq = m * dec[c, NQ : NQ + 1, :] * rinv
            et = m * mq
            rate = mq * (2.0 + (0.5 * m) * (1.0 - 0.25 * g) * isq)
            terms = [et, et * isq * (g * (1.0 + arg)) * bj, rate * dx, rate * dy, rate * dz]
            acc = terms if acc is None else [a + t for a, t in zip(acc, terms)]
        for q in range(5):
            keep_sum(pair, q, r, acc[q])


def second_columns(me, dec, born, colb):
    spread_columns(
        [dec[me, q : q + 1, :] for q in (OX, NY, NZ)]
        + [born[me, 0:1, :], 0.25 * born[me, 1:2, :]],
        colb,
    )


def second_own_kernel(side, dec, bead, part, colb, pair, born):
    for o in range(8):
        c = own_cell(o)
        born[c, 0:1, :] = bead[0, o : o + 1, :]
        born[c, 1:2, :] = 1.0 / bead[0, o : o + 1, :]
    for v in range(4):
        o = side * 4 + v
        second_columns(own_cell(o), dec, born, colb)
        second_blocks([own_cell(p) for p in near_own(o)], True, dec, born, colb, pair)
        for q in range(5):
            part[v, q : q + 1, :] = row_sum(pair, q)


def second_halo_kernel(
    dec, bead, xlow, xhigh, yrow, part0, part1, act, message, parts, mix, outw, factor,
    grad_psi, grad_message, direct, mix_out, colb, pair, born, sums,
):
    for c in range(20):
        ex, v = c // 5, c % 5
        if v == 4:
            row = yrow[ex : ex + 1, :]
        elif ex in (1, 2):
            row = bead[0, (ex - 1) * 4 + v : (ex - 1) * 4 + v + 1, :]
        else:
            row = (xlow if ex == 0 else xhigh)[v : v + 1, :]
        row = jnp.where(dec[c, NVALID : NVALID + 1, :] > 0.0, row, 1.0)
        born[c, 0:1, :] = row
        born[c, 1:2, :] = 1.0 / row
    for o in range(8):
        second_columns(own_cell(o), dec, born, colb)
        second_blocks(near_halo(o), False, dec, born, colb, pair)
        before = (part0, part1)[o // 4]
        for q in range(5):
            sums[o, q : q + 1, :] = row_sum(pair, q) + before[o % 4, q : q + 1, :]
    total = [gather_rows(sums, q) for q in range(5)]
    cells = [own_cell(o) for o in range(8)]
    charge = jnp.concatenate([dec[c, NQ : NQ + 1, :] for c in cells], axis=0)
    valid = jnp.concatenate([dec[c, NVALID : NVALID + 1, :] for c in cells], axis=0)
    inv = 1.0 / bead[0]
    scaled = SOLVENT * charge
    self_energy = scaled * charge * valid * inv
    energy = scaled * total[0] + self_energy
    grad_born = -scaled * total[1] - self_energy * inv
    for d in range(3):
        direct[d] = -4.0 * scaled * total[2 + d]
    tanh_screen, tanh_corr, rho = bead[1], bead[2], bead[3]
    down = 1.0 - 0.8 * tanh_screen
    psi = (
        SCREEN_GAIN * rho * grad_born * rho * (1.0 + 0.5 * tanh_corr) * 0.8
        * (1.0 - tanh_screen * tanh_screen) / (down * down)
    )
    grad_psi[...] = psi
    grad_corr = grad_born * rho * 0.5 * (1.0 - tanh_corr * tanh_corr) / down
    corr_cols = jnp.transpose(grad_corr)
    weight = outw[...]
    kind = lax.broadcasted_iota(jnp.int32, (32, SLOTS), 0)
    lane = lax.broadcasted_iota(jnp.int32, (32, SLOTS), 1)
    mix_sum = None
    for o in range(8):
        col = corr_cols[:, o : o + 1]
        hidden = act[o]
        grad_hidden = (col * weight * (1.0 - hidden * hidden)).astype(BF16)
        grad_message[o] = lax.dot_general(
            grad_hidden, mix[...], (((1,), (1,)), ((), ())), preferred_element_type=F32
        ).astype(BF16)
        term = lax.dot_general(
            message[o], grad_hidden, (((0,), (0,)), ((), ())), preferred_element_type=F32
        )
        out_term = jnp.sum(col * hidden, axis=0, keepdims=True)
        scale_term = psi[o : o + 1] * parts[o]
        if mix_sum is None:
            mix_sum, out_sum, scale_sum = term, out_term, scale_term
        else:
            mix_sum = mix_sum + term
            out_sum = out_sum + out_term
            scale_sum = scale_sum + scale_term
    mix_out[0:SLOTS, :] = mix_sum
    both = jnp.sum(jnp.sum(energy, axis=0, keepdims=True), axis=1, keepdims=True)
    scale_col = jnp.sum(scale_sum, axis=1, keepdims=True)
    scale_row = jnp.sum(jnp.where(kind == lane, scale_col, 0.0), axis=0, keepdims=True)
    scale_row = scale_row * factor[...]
    mix_out[SLOTS:, :] = jnp.concatenate(
        [out_sum, jnp.broadcast_to(both, (1, SLOTS)), scale_row, jnp.zeros((5, SLOTS), F32)],
        axis=0,
    )


def fold8(value):
    total = value[0:8]
    for r in range(8, value.shape[0], 8):
        total = total + value[r : r + 8]
    return total


def third_kernel(
    first, count, xlow, low, high, xhigh, yrow, dec, grad_psi, grad_message,
    out, colb, pair, jacc, inner,
):
    refs = (xlow, low, high, xhigh, yrow)
    for k in range(count):
        o = first + k
        me = own_cell(o)
        cells = [ex * 5 + v for ex, v in near_all(o)]
        spread_columns(
            [dec[me, q : q + 1, :] for q in (OX, NY, NZ, ORHO2)] + [grad_psi[o : o + 1, :]], colb
        )
        gmsg = grad_message[o]
        for n, c in enumerate(cells):
            inner[n] = lax.dot_general(
                gmsg, cell_source(refs, c)[0:SLOTS, :], (((1,), (1,)), ((), ())),
                preferred_element_type=F32,
            )
        for r in range(0, SLOTS, CHUNK):
            sl = pl.ds(r, CHUNK)
            xi, yi, zi, ri2, gp = (colb[q, sl, :] for q in range(5))
            acc = None
            for n, c in enumerate(cells):
                dx = xi - dec[c, NX : NX + 1, :]
                dy = yi - dec[c, NY : NY + 1, :]
                dz = zi - dec[c, NZ : NZ + 1, :]
                s = dx * dx + dy * dy + dz * dz
                if n == 0:
                    s = s + self_far(r, CHUNK)
                m = jnp.maximum(1.0 - s, 0.0)
                inv = 1.0 / (s + dec[c, NR2 : NR2 + 1, :] + ri2)
                slope = dec[c, NR3 : NR3 + 1, :] * (inv * inv) * gp * (1.0 + m * inv)
                gauss = jnp.exp(-4.0 * s) * (1.0 + 2.0 * m) * inner[n, sl, :]
                rate = m * (slope + gauss)
                terms = [rate * dx, rate * dy, rate * dz]
                acc = terms if acc is None else [a + t for a, t in zip(acc, terms)]
                for d in range(3):
                    folded = fold8(terms[d])
                    if r == 0:
                        jacc[n, d] = folded
                    else:
                        jacc[n, d] += folded
            for d in range(3):
                keep_sum(pair, d, r, acc[d])
        for d in range(3):
            for n in range(len(cells)):
                out[k, d, n : n + 1, :] = jnp.sum(jacc[n, d], axis=0, keepdims=True)
            for n in range(len(cells), 9):
                out[k, d, n : n + 1, :] = jnp.zeros((1, SLOTS), F32)
            out[k, d, 9:10, :] = row_sum(pair, d)
            out[k, d, 10:16, :] = jnp.zeros((6, SLOTS), F32)


def gather_kernel(count, *refs):
    pieces, direct, core, edge = refs[: 8 // count], refs[-3], refs[-2], refs[-1]
    for ex in range(4):
        for v in range(5):
            for d in range(3):
                value = None
                for o in range(8):
                    near = near_all(o)
                    if (ex, v) not in near:
                        continue
                    n = near.index((ex, v))
                    term = pieces[o // count][o % count, d, n : n + 1, :]
                    value = term if value is None else value + term
                value = -4.0 * value
                if ex in (1, 2) and v < 4:
                    o = (ex - 1) * 4 + v
                    value = value - direct[d, o : o + 1, :]
                    value = value + 4.0 * pieces[o // count][o % count, d, 9:10, :]
                if v == 4:
                    edge[d * 4 + ex : d * 4 + ex + 1, :] = value
                else:
                    core[ex, d, v : v + 1, :] = value
    edge[12:16, :] = jnp.zeros((4, SLOTS), F32)


def weigh_kernel(slots, targets, sums, out):
    core = lax.axis_index("gy") % 2
    row = sums[SLOTS + 1 : SLOTS + 2, :]
    target = jnp.where(core == 0, targets[0], targets[1])
    weight = (row * (1.0 / slots) - target) * (1.0 / math.sqrt(slots))
    out[...] = sums[...] * weight
    out[SLOTS + 1 : SLOTS + 2, :] = row


def finish_kernel(slots, scaled, partner, stay, *refs):
    outs, staged, sem = refs[:5], refs[5:10], refs[10]
    energies, forces, grad_mix, grad_out, grad_scale = staged
    seat = lax.axis_index("gy")
    core, upper = seat % 2, seat // 2
    for d in range(3):
        for x in range(2):
            for y in range(2):
                row = upper if y == 0 else 1 - upper
                k = SLOTS + 8 + d * 4 + x * 2 + y
                forces[d, core, x, pl.ds(row, 1), :] = stay[d, x, pl.ds(y, 1), :]
                forces[d, 1 - core, x, pl.ds(row, 1), :] = partner[k : k + 1, :]
    grad_mix[...] = scaled[0:SLOTS, :] + partner[0:SLOTS, :]
    grad_out[...] = scaled[SLOTS : SLOTS + 1, :] + partner[SLOTS : SLOTS + 1, :]
    both = scaled[SLOTS + 2 : SLOTS + 3, :] + partner[SLOTS + 2 : SLOTS + 3, :]
    grad_scale[...] = both[:, 0:32]
    lane = lax.broadcasted_iota(jnp.int32, (1, SLOTS), 1)
    mine, theirs = scaled[SLOTS + 1 : SLOTS + 2, :], partner[SLOTS + 1 : SLOTS + 2, :]
    energies[...] = (jnp.where(lane == core, mine, theirs) * (1.0 / slots))[:, 0:2]
    copies = [pltpu.make_async_copy(a, b, sem.at[i]) for i, (a, b) in enumerate(zip(staged, outs))]
    for copy in copies:
        copy.start()
    for copy in copies:
        copy.wait()


def vmem(count):
    return [pl.BlockSpec(memory_space=pltpu.VMEM)] * count


def smem(count):
    return [pl.BlockSpec(memory_space=pltpu.SMEM)] * count


def shape(*dims, dtype=F32):
    return jax.ShapeDtypeStruct(dims, dtype)


def square(*lead, dtype=F32):
    return pltpu.VMEM(lead + (SLOTS, SLOTS), dtype)


def call(kernel, name, in_specs, out_shape, scratch, flops=1000000):
    single = not isinstance(out_shape, tuple)
    return pl.pallas_call(
        kernel,
        name=name,
        in_specs=in_specs,
        out_specs=vmem(1)[0] if single else tuple(vmem(len(out_shape))),
        out_shape=out_shape,
        scratch_shapes=scratch,
        compiler_params=pltpu.CompilerParams(vmem_limit_bytes=40 << 20),
        cost_estimate=pl.CostEstimate(flops=flops, transcendentals=0, bytes_accessed=1 << 20),
    )


def chain(axis):
    count = lax.axis_size(axis)
    forward = [(i, i + 1) for i in range(count - 1)]
    return forward, [(b, a) for a, b in forward]


def exchange(low, high, axis):
    forward, backward = chain(axis)
    return lax.ppermute(high, axis, forward), lax.ppermute(low, axis, backward)


def flip(value, axis, bit):
    return lax.ppermute(value, axis, [(i, i ^ bit) for i in range(lax.axis_size(axis))])


PIECE = 2


def on_device(
    positions, charges, slot_bead_types, cell_counts, features,
    radius_table, scale_table, mix_weight, out_weight, targets,
):
    total_slots = 2 * lax.axis_size("gx") * 2 * lax.axis_size("gy") * SLOTS
    seat = lax.axis_index("gy")
    core, upper = seat % 2, seat // 2
    inner = (core ^ upper) == 0
    half = shape(2, 2, ROWS, SLOTS, dtype=BF16)
    big = [
        pltpu.with_memory_space_constraint(v, pltpu.HBM)
        for v in (cell_counts, radius_table, scale_table, positions, charges, slot_bead_types, features, mix_weight,
                  out_weight.reshape(1, SLOTS))
    ]
    kept, sent, mix, outw, factor = call(
        pack_kernel, "pack", [pl.BlockSpec(memory_space=pltpu.HBM)] * 9,
        (half, half, shape(SLOTS, SLOTS, dtype=BF16), shape(1, SLOTS), shape(1, SLOTS)),
        [pltpu.SMEM((2, 2, 2), jnp.int32), pltpu.SMEM((32,), F32), pltpu.SMEM((32,), F32),
         pltpu.VMEM((3, 2, 2, 2, SLOTS), F32), pltpu.VMEM((2, 2, 2, SLOTS), F32),
         pltpu.VMEM((2, 2, 2, SLOTS), jnp.int32), square(2, 2, 2, dtype=BF16),
         pltpu.SemaphoreType.DMA((9,))],
        10000,
    )(*big)
    got = flip(sent, "gy", 1)
    low, high = (
        jnp.concatenate([jnp.where(inner, kept[x], got[x]), jnp.where(inner, got[x], kept[x])])
        for x in range(2)
    )

    xlow, xhigh = exchange(low, high, "gx")
    state = (shape(8, SLOTS, SLOTS), shape(8, 32, SLOTS), shape(8, 8, SLOTS))
    code, hots = shape(20, 16, SLOTS), shape(20, 32, SLOTS, dtype=BF16)
    started = call(
        first_own_kernel, "first_own", vmem(2), state,
        [pltpu.VMEM((8, 16, SLOTS), F32), pltpu.VMEM((8, 32, SLOTS), BF16), square(4),
         square(6, dtype=BF16), square(6, dtype=BF16), square(1, 2, dtype=BF16)],
    )(low, high)
    xlow, xhigh, low, high, started = lax.optimization_barrier((xlow, xhigh, low, high, started))
    yrow = flip(jnp.stack([xlow[3], low[3], high[3], xhigh[3]]), "gy", 2)
    dec, hot, *started = call(
        first_side_kernel, "first_side", vmem(7), (code, hots) + state,
        [square(4), square(5, dtype=BF16), square(5, dtype=BF16), square(1, 2, dtype=BF16)],
    )(xlow, low, high, xhigh, *started)
    dec, bead, act, message, parts = call(
        first_halo_kernel, "first_halo", vmem(8),
        (code, shape(4, 8, SLOTS), shape(8, SLOTS, SLOTS),
         shape(8, SLOTS, SLOTS, dtype=BF16), shape(8, 32, SLOTS)),
        [pltpu.VMEM((20, 32, SLOTS), BF16), square(4), square(5, dtype=BF16),
         square(5, dtype=BF16), square(2, 2, dtype=BF16), pltpu.VMEM((8, 8, SLOTS), F32)],
    )(dec, hot, yrow, *started, mix, outw)

    def second_own(side, dec, bead):
        return call(
            lambda *refs: second_own_kernel(side, *refs), f"second_own{side}", vmem(2),
            shape(4, 8, SLOTS),
            [square(5), square(5, 2, dtype=BF16), pltpu.VMEM((20, 8, SLOTS), F32)],
        )(dec, bead)

    born = bead[0]
    bxlow, bxhigh = exchange(born[0:4], born[4:8], "gx")
    sums0 = second_own(0, dec, bead)
    bxlow, bxhigh, bead, sums0 = lax.optimization_barrier((bxlow, bxhigh, bead, sums0))
    byrow = flip(jnp.stack([bxlow[3], born[3], born[7], bxhigh[3]]), "gy", 2)
    sums1 = second_own(1, dec, bead)

    grad_psi, grad_message, direct, sums = call(
        second_halo_kernel, "second_halo", vmem(13),
        (shape(8, SLOTS), shape(8, SLOTS, SLOTS, dtype=BF16), shape(3, 8, SLOTS),
         shape(SLOTS + 8, SLOTS)),
        [square(5), square(5, 2, dtype=BF16), pltpu.VMEM((20, 8, SLOTS), F32),
         pltpu.VMEM((8, 8, SLOTS), F32)],
    )(dec, bead, bxlow, bxhigh, byrow, sums0, sums1, act, message, parts, mix, outw, factor)

    def third(first, grad_psi):
        return call(
            lambda *refs: third_kernel(first, PIECE, *refs), f"third{first}", vmem(8),
            shape(PIECE, 3, 16, SLOTS),
            [square(5), square(3, 2, dtype=BF16), pltpu.VMEM((9, 3, 8, SLOTS), F32), square(9)],
        )(xlow, low, high, xhigh, yrow, dec, grad_psi, grad_message)

    bits = []
    bit = 1
    while bit < lax.axis_size("gx"):
        bits.append(bit)
        bit *= 2
    pieces = []
    for bit in bits[1:5]:
        other = flip(sums, "gx", bit)
        piece = third(PIECE * len(pieces), grad_psi)
        other, grad_psi, piece = lax.optimization_barrier((other, grad_psi, piece))
        pieces.append(piece)
        sums = sums + other
    block, edge = call(
        lambda *refs: gather_kernel(PIECE, *refs), "gather", vmem(8 // PIECE + 1),
        (shape(4, 3, 4, SLOTS), shape(16, SLOTS)), [],
    )(*pieces, direct)
    joint = jnp.concatenate([sums, edge])
    other = flip(joint, "gy", 2)
    sums = sums + other[: SLOTS + 8]
    block = block.at[:, :, 3].add(jnp.swapaxes(other[SLOTS + 8 : SLOTS + 20].reshape(3, 4, SLOTS), 0, 1))
    even = lax.axis_index("gx") % 2 == 0
    facing, away = jnp.where(even, block[3], block[0]), jnp.where(even, block[0], block[3])
    count = lax.axis_size("gx")
    pairs = [(i, i + 1) for i in range(1, count - 1, 2)]
    outer = lax.ppermute(away, "gx", pairs + [(j, i) for i, j in pairs])
    other = flip(jnp.concatenate([sums, facing.reshape(12, SLOTS)]), "gx", 1)
    sums = sums + other[: SLOTS + 8]
    near = other[SLOTS + 8 :].reshape(3, 4, SLOTS)
    for bit in bits[5:]:
        sums = sums + flip(sums, "gx", bit)
    own = jnp.stack(
        [block[1] + jnp.where(even, outer, near), block[2] + jnp.where(even, near, outer)], axis=1
    )
    own = own.reshape(3, 2, 2, 2, SLOTS)
    front, back = own[:, :, 0], own[:, :, 1]
    stay, leave = jnp.where(inner, front, back), jnp.where(inner, back, front)

    scaled = call(
        lambda *refs: weigh_kernel(total_slots, *refs), "weigh", smem(1) + vmem(1),
        shape(SLOTS + 8, SLOTS), [], 1000,
    )(targets, sums)
    partner = flip(jnp.concatenate([scaled, leave.reshape(12, SLOTS)]), "gy", 1)
    outs = (shape(1, 2), shape(3, 2, 2, 2, SLOTS), shape(SLOTS, SLOTS), shape(1, SLOTS), shape(1, 32))
    energies, forces, grad_mix, grad_out, grad_scale = pl.pallas_call(
        lambda *refs: finish_kernel(total_slots, *refs),
        name="finish",
        in_specs=vmem(3),
        out_specs=tuple([pl.BlockSpec(memory_space=pltpu.HBM)] * 5),
        out_shape=outs,
        scratch_shapes=[pltpu.VMEM(o.shape, F32) for o in outs] + [pltpu.SemaphoreType.DMA((5,))],
        compiler_params=pltpu.CompilerParams(vmem_limit_bytes=8 << 20),
    )(scaled, partner, stay)
    return (
        energies.reshape(2), forces, grad_mix, grad_out.reshape(SLOTS), grad_scale.reshape(32)
    )


def solution(mesh):
    placed = (
        P(None, None, "gx", "gy", None),
        P(None, "gx", "gy", None),
        P(None, "gx", "gy", None),
        P(None, "gx", "gy"),
        P(None, "gx", "gy", None, None),
        P(),
        P(),
        P(),
        P(),
        P(),
    )
    return jax.shard_map(
        on_device,
        mesh=mesh,
        in_specs=placed,
        out_specs=(P(), P(None, None, "gx", "gy", None), P(), P(), P()),
        check_vma=False,
    )
```

```python
import math

import jax
import jax.numpy as jnp
from jax import lax
from jax.experimental import pallas as pl
from jax.experimental.pallas import tpu as pltpu
from jax.sharding import PartitionSpec as P

SOLVENT = -0.5 * 0.98726
SCREEN_GAIN = 12.0
FAR = 4096.0
SLOTS = 128
ROWS = 160
CHUNK = 32
F32 = jnp.float32
BF16 = jnp.bfloat16


def split3(row):
    high = row.astype(BF16).astype(F32)
    rest = row - high
    mid = rest.astype(BF16).astype(F32)
    return [high, mid, rest - mid]


def pack_kernel(
    count_any, radius_any, scale_any, pos_any, charge_any, kind_any, feat_any, mix_any, outw_any,
    kept, sent, mix_out, outw_out, factor_out, counts, radius, scale, pos, charge, kind, feat, sem,
):
    copies = [
        pltpu.make_async_copy(src, dst, sem.at[i])
        for i, (src, dst) in enumerate(
            (
                (pos_any, pos),
                (charge_any, charge),
                (kind_any, kind),
                (feat_any, feat),
                (mix_any, mix_out),
                (outw_any, outw_out),
                (count_any, counts),
                (radius_any, radius),
                (scale_any, scale),
            )
        )
    ]
    for copy in copies:
        copy.start()
    for copy in copies:
        copy.wait()
    place = lax.axis_index("gy")
    core = place % 2
    upper = place // 2
    slot = lax.broadcasted_iota(jnp.int32, (1, SLOTS), 1)
    zero = jnp.zeros((1, SLOTS), F32)
    spots = [(s, x, y) for s in range(2) for x in range(2) for y in range(2)]

    def seat(s, y):
        frame = core if s == 0 else 1 - core
        row = upper if y == 0 else 1 - upper
        return frame, row

    found = []
    for s, x, y in spots:
        frame, row = seat(s, y)
        found.append(kind[frame, x, pl.ds(row, 1), :])
    kinds = jnp.concatenate(found, axis=0)
    rho = jnp.zeros((8, SLOTS), F32)
    factor = jnp.zeros((8, SLOTS), F32)
    for k in range(32):
        rho = jnp.where(kinds == k, radius[k], rho)
        factor = jnp.where(kinds == k, scale[k], factor)
    reach = rho * factor
    weights = jnp.zeros((1, SLOTS), F32)
    for k in range(32):
        span = radius[k] * scale[k]
        weights = jnp.where(slot == k, radius[k] * span * span, weights)
    factor_out[...] = weights
    for o, (s, x, y) in enumerate(spots):
        frame, row = seat(s, y)
        out = (kept, sent)[s]
        rows = []
        for d in range(3):
            rows += split3(pos[d, frame, x, pl.ds(row, 1), :])
        rows += split3(charge[frame, x, pl.ds(row, 1), :])
        rows += split3(rho[o : o + 1])
        rows += split3(reach[o : o + 1])
        rows.append(kinds[o : o + 1].astype(F32))
        rows.append((slot < counts[frame, x, row]).astype(F32))
        rows += [zero] * (32 - len(rows))
        out[x, y, 0:SLOTS, :] = feat[frame, x, row]
        out[x, y, SLOTS:ROWS, :] = jnp.concatenate(rows, axis=0).astype(BF16)


def chooser():
    r = lax.broadcasted_iota(jnp.int32, (16, 32), 0)
    k = lax.broadcasted_iota(jnp.int32, (16, 32), 1)
    triple = (r < 6) & (k >= 3 * r) & (k < 3 * r + 3)
    single = ((r == 6) | (r == 7)) & (k == r + 12)
    return jnp.where(triple | single, 1.0, 0.0).astype(BF16)


def decode(pick, coded):
    return jnp.dot(pick, coded, preferred_element_type=F32)


def near_rows(got):
    valid = got[7:8] > 0.0
    reach = got[5:6]
    square = reach * reach
    return [
        jnp.where(valid, got[0:1], -FAR),
        got[1:2],
        got[2:3],
        got[3:4],
        square,
        square * reach,
        got[4:5],
        got[6:7],
        got[7:8],
        jnp.where(valid, got[0:1], FAR),
        got[4:5] * got[4:5],
    ]


NX, NY, NZ, NQ, NR2, NR3, NRHO, NKIND, NVALID, OX, ORHO2 = range(11)


def spread_columns(rows, out):
    pad = [jnp.zeros((1, SLOTS), F32)] * (8 - len(rows))
    cols = jnp.transpose(jnp.concatenate(rows + pad, axis=0))
    for q in range(len(rows)):
        out[q] = jnp.broadcast_to(cols[:, q : q + 1], (SLOTS, SLOTS))


def self_far(start, size):
    r = lax.broadcasted_iota(jnp.int32, (size, SLOTS), 0) + start
    c = lax.broadcasted_iota(jnp.int32, (size, SLOTS), 1)
    return jnp.where(r == c, FAR * FAR, 0.0)


def keep_sum(pair, q, start, value):
    size = value.shape[0]
    high = value.astype(BF16)
    pair[q, 0, pl.ds(start, size), :] = high
    pair[q, 1, pl.ds(start, size), :] = (value - high.astype(F32)).astype(BF16)


def row_sum(pair, q):
    ones = jnp.ones((8, SLOTS), BF16)
    dims = (((1,), (1,)), ((), ()))
    high = lax.dot_general(ones, pair[q, 0], dims, preferred_element_type=F32)
    low = lax.dot_general(ones, pair[q, 1], dims, preferred_element_type=F32)
    return (high + low)[0:1]


def own_cell(o):
    return (o // 4 + 1) * 5 + o % 4


def near_own(o):
    x, v = o // 4, o % 4
    rows = [w for w in (v, v - 1, v + 1) if 0 <= w < 4]
    return [x * 4 + w for w in rows] + [(1 - x) * 4 + w for w in rows]


def near_halo(o):
    x, v = o // 4, o % 4
    cells = [15 * x + w for w in (v - 1, v, v + 1) if w >= 0]
    return cells + ([9, 14] if v == 3 else [])


def near_all(o):
    x, v = o // 4, o % 4
    spots = [(0, 0)] + [(p, q) for p in (-1, 0, 1) for q in (-1, 0, 1) if (p, q) != (0, 0)]
    return [(x + 1 + p, v + q) for p, q in spots if v + q >= 0]


def gather_rows(ref, q, count=8):
    return jnp.concatenate([ref[o, q : q + 1, :] for o in range(count)], axis=0)


def unpack(pick, coded, c, dec, hot):
    rows = near_rows(decode(pick, coded))
    for q, row in enumerate(rows):
        dec[c, q : q + 1, :] = row
    kinds = lax.broadcasted_iota(jnp.int32, (32, SLOTS), 0).astype(F32)
    hot[c] = jnp.where(kinds == rows[NKIND], 1.0, 0.0).astype(BF16)


def first_blocks(cells, with_self, dec, feat, hot, colb, wgt, scl, pair, message, parts):
    size = CHUNK
    for r in range(0, SLOTS, size):
        sl = pl.ds(r, size)
        xi, yi, zi, ri2 = (colb[q, sl, :] for q in range(4))
        acc = None
        for n, c in enumerate(cells):
            rj2 = dec[c, NR2 : NR2 + 1, :]
            dx = xi - dec[c, NX : NX + 1, :]
            dy = yi - dec[c, NY : NY + 1, :]
            dz = zi - dec[c, NZ : NZ + 1, :]
            s = dx * dx + dy * dy + dz * dz
            if with_self and n == 0:
                s = s + self_far(r, size)
            m = jnp.maximum(1.0 - s, 0.0)
            t = m * m
            inv = 1.0 / (s + rj2 + ri2)
            ti = t * (inv * inv)
            term = ti * dec[c, NR3 : NR3 + 1, :]
            acc = term if acc is None else acc + term
            wgt[n, sl, :] = (t * jnp.exp(-4.0 * s)).astype(BF16)
            scl[n, sl, :] = (ti * (3.0 - (4.0 * rj2) * inv)).astype(BF16)
        keep_sum(pair, 0, r, acc)
    for n, c in enumerate(cells):
        term = jnp.dot(wgt[n], feat(c), preferred_element_type=F32)
        part = lax.dot_general(
            hot[c], scl[n], (((1,), (1,)), ((), ())), preferred_element_type=F32
        )
        message = term if message is None else message + term
        parts = part if parts is None else parts + part
    return message, parts


def first_own_kernel(low, high, msg_out, part_out, scr_out, dec, hot, colb, wgt, scl, pair):
    pick = chooser()
    for x in range(2):
        for v in range(4):
            unpack(pick, (low, high)[x][v, SLOTS:ROWS, :], x * 4 + v, dec, hot)
    for o in range(8):
        spread_columns([dec[o, q : q + 1, :] for q in (OX, NY, NZ, ORHO2)], colb)
        message, parts = first_blocks(
            near_own(o), True, dec, lambda c: (low, high)[c // 4][c % 4, 0:SLOTS, :],
            hot, colb, wgt, scl, pair, None, None,
        )
        msg_out[o] = message
        part_out[o] = parts
        scr_out[o] = jnp.broadcast_to(row_sum(pair, 0), (8, SLOTS))


def cell_source(refs, c):
    ex, v = c // 5, c % 5
    return refs[4].at[ex] if v == 4 else refs[ex].at[v]


def first_side_kernel(
    xlow, low, high, xhigh, msg_in, part_in, scr_in,
    dec, hot, msg_out, part_out, scr_out, colb, wgt, scl, pair,
):
    pick = chooser()
    refs = (xlow, low, high, xhigh)
    for ex in range(4):
        for v in range(4):
            unpack(pick, refs[ex][v, SLOTS:ROWS, :], ex * 5 + v, dec, hot)
        dec[ex * 5 + 4] = jnp.zeros((16, SLOTS), F32)
        hot[ex * 5 + 4] = jnp.zeros((32, SLOTS), BF16)
    for o in range(8):
        me = own_cell(o)
        spread_columns([dec[me, q : q + 1, :] for q in (OX, NY, NZ, ORHO2)], colb)
        message, parts = first_blocks(
            [c for c in near_halo(o) if c % 5 != 4], False, dec,
            lambda c: refs[c // 5][c % 5, 0:SLOTS, :],
            hot, colb, wgt, scl, pair, msg_in[o], part_in[o],
        )
        msg_out[o] = message
        part_out[o] = parts
        scr_out[o] = scr_in[o] + row_sum(pair, 0)


def first_halo_kernel(
    dec_in, hot_in, yrow, msg_in, part_in, scr_in, mix, outw,
    dec, bead, act_out, msg_out, part_out, hot, colb, wgt, scl, pair, sums,
):
    pick = chooser()
    dec[...] = dec_in[...]
    hot[...] = hot_in[...]
    for ex in range(4):
        unpack(pick, yrow[ex, SLOTS:ROWS, :], ex * 5 + 4, dec, hot)
    weight = outw[...]
    for o in range(8):
        me = own_cell(o)
        message, parts = msg_in[o], part_in[o]
        screen = scr_in[o, 0:1, :]
        if o % 4 == 3:
            spread_columns([dec[me, q : q + 1, :] for q in (OX, NY, NZ, ORHO2)], colb)
            message, parts = first_blocks(
                [c for c in near_halo(o) if c % 5 == 4], False, dec,
                lambda c: yrow[c // 5, 0:SLOTS, :],
                hot, colb, wgt, scl, pair, message, parts,
            )
            screen = screen + row_sum(pair, 0)
        part_out[o] = parts
        message = message.astype(BF16)
        msg_out[o] = message
        act = jnp.tanh(jnp.dot(message, mix[...], preferred_element_type=F32))
        act_out[o] = act
        keep_sum(pair, 1, 0, act * weight)
        sums[o, 0:1, :] = screen
        sums[o, 1:2, :] = row_sum(pair, 1)
    cells = [own_cell(o) for o in range(8)]
    rho = jnp.concatenate([dec[c, NRHO : NRHO + 1, :] for c in cells], axis=0)
    valid = jnp.concatenate([dec[c, NVALID : NVALID + 1, :] for c in cells], axis=0)
    tanh_screen = jnp.tanh(SCREEN_GAIN * rho * gather_rows(sums, 0))
    tanh_corr = jnp.tanh(gather_rows(sums, 1))
    born = rho * (1.0 + 0.5 * tanh_corr) / (1.0 - 0.8 * tanh_screen)
    bead[0] = jnp.where(valid > 0.0, born, 1.0)
    bead[1] = tanh_screen
    bead[2] = tanh_corr
    bead[3] = rho


def second_blocks(cells, with_self, dec, born, colb, pair):
    size = CHUNK // 2
    for r in range(0, SLOTS, size):
        sl = pl.ds(r, size)
        xi, yi, zi, bi, ibi = (colb[q, sl, :] for q in range(5))
        acc = None
        for n, c in enumerate(cells):
            bj = born[c, 0:1, :]
            dx = xi - dec[c, NX : NX + 1, :]
            dy = yi - dec[c, NY : NY + 1, :]
            dz = zi - dec[c, NZ : NZ + 1, :]
            s = dx * dx + dy * dy + dz * dz
            if with_self and n == 0:
                s = s + self_far(r, size)
            m = jnp.maximum(1.0 - s, 0.0)
            arg = s * (ibi * born[c, 1:2, :])
            g = jnp.exp(-arg)
            rinv = lax.rsqrt(s + bi * bj * g)
            isq = rinv * rinv
            mq = m * dec[c, NQ : NQ + 1, :] * rinv
            et = m * mq
            rate = mq * (2.0 + (0.5 * m) * (1.0 - 0.25 * g) * isq)
            terms = [et, et * isq * (g * (1.0 + arg)) * bj, rate * dx, rate * dy, rate * dz]
            acc = terms if acc is None else [a + t for a, t in zip(acc, terms)]
        for q in range(5):
            keep_sum(pair, q, r, acc[q])


def second_columns(me, dec, born, colb):
    spread_columns(
        [dec[me, q : q + 1, :] for q in (OX, NY, NZ)]
        + [born[me, 0:1, :], 0.25 * born[me, 1:2, :]],
        colb,
    )


def second_own_kernel(side, dec, bead, part, colb, pair, born):
    for o in range(8):
        c = own_cell(o)
        born[c, 0:1, :] = bead[0, o : o + 1, :]
        born[c, 1:2, :] = 1.0 / bead[0, o : o + 1, :]
    for v in range(4):
        o = side * 4 + v
        second_columns(own_cell(o), dec, born, colb)
        second_blocks([own_cell(p) for p in near_own(o)], True, dec, born, colb, pair)
        for q in range(5):
            part[v, q : q + 1, :] = row_sum(pair, q)


def second_halo_kernel(
    dec, bead, xlow, xhigh, yrow, part0, part1, act, message, parts, mix, outw, factor,
    grad_psi, grad_message, direct, mix_out, colb, pair, born, sums,
):
    for c in range(20):
        ex, v = c // 5, c % 5
        if v == 4:
            row = yrow[ex : ex + 1, :]
        elif ex in (1, 2):
            row = bead[0, (ex - 1) * 4 + v : (ex - 1) * 4 + v + 1, :]
        else:
            row = (xlow if ex == 0 else xhigh)[v : v + 1, :]
        row = jnp.where(dec[c, NVALID : NVALID + 1, :] > 0.0, row, 1.0)
        born[c, 0:1, :] = row
        born[c, 1:2, :] = 1.0 / row
    for o in range(8):
        second_columns(own_cell(o), dec, born, colb)
        second_blocks(near_halo(o), False, dec, born, colb, pair)
        before = (part0, part1)[o // 4]
        for q in range(5):
            sums[o, q : q + 1, :] = row_sum(pair, q) + before[o % 4, q : q + 1, :]
    total = [gather_rows(sums, q) for q in range(5)]
    cells = [own_cell(o) for o in range(8)]
    charge = jnp.concatenate([dec[c, NQ : NQ + 1, :] for c in cells], axis=0)
    valid = jnp.concatenate([dec[c, NVALID : NVALID + 1, :] for c in cells], axis=0)
    inv = 1.0 / bead[0]
    scaled = SOLVENT * charge
    self_energy = scaled * charge * valid * inv
    energy = scaled * total[0] + self_energy
    grad_born = -scaled * total[1] - self_energy * inv
    for d in range(3):
        direct[d] = -4.0 * scaled * total[2 + d]
    tanh_screen, tanh_corr, rho = bead[1], bead[2], bead[3]
    down = 1.0 - 0.8 * tanh_screen
    psi = (
        SCREEN_GAIN * rho * grad_born * rho * (1.0 + 0.5 * tanh_corr) * 0.8
        * (1.0 - tanh_screen * tanh_screen) / (down * down)
    )
    grad_psi[...] = psi
    grad_corr = grad_born * rho * 0.5 * (1.0 - tanh_corr * tanh_corr) / down
    corr_cols = jnp.transpose(grad_corr)
    weight = outw[...]
    kind = lax.broadcasted_iota(jnp.int32, (32, SLOTS), 0)
    lane = lax.broadcasted_iota(jnp.int32, (32, SLOTS), 1)
    mix_sum = None
    for o in range(8):
        col = corr_cols[:, o : o + 1]
        hidden = act[o]
        grad_hidden = (col * weight * (1.0 - hidden * hidden)).astype(BF16)
        grad_message[o] = lax.dot_general(
            grad_hidden, mix[...], (((1,), (1,)), ((), ())), preferred_element_type=F32
        ).astype(BF16)
        term = lax.dot_general(
            message[o], grad_hidden, (((0,), (0,)), ((), ())), preferred_element_type=F32
        )
        out_term = jnp.sum(col * hidden, axis=0, keepdims=True)
        scale_term = psi[o : o + 1] * parts[o]
        if mix_sum is None:
            mix_sum, out_sum, scale_sum = term, out_term, scale_term
        else:
            mix_sum = mix_sum + term
            out_sum = out_sum + out_term
            scale_sum = scale_sum + scale_term
    mix_out[0:SLOTS, :] = mix_sum
    both = jnp.sum(jnp.sum(energy, axis=0, keepdims=True), axis=1, keepdims=True)
    scale_col = jnp.sum(scale_sum, axis=1, keepdims=True)
    scale_row = jnp.sum(jnp.where(kind == lane, scale_col, 0.0), axis=0, keepdims=True)
    scale_row = scale_row * factor[...]
    mix_out[SLOTS:, :] = jnp.concatenate(
        [out_sum, jnp.broadcast_to(both, (1, SLOTS)), scale_row, jnp.zeros((5, SLOTS), F32)],
        axis=0,
    )


def fold8(value):
    total = value[0:8]
    for r in range(8, value.shape[0], 8):
        total = total + value[r : r + 8]
    return total


def third_kernel(
    first, count, xlow, low, high, xhigh, yrow, dec, grad_psi, grad_message,
    out, colb, pair, jacc, inner,
):
    refs = (xlow, low, high, xhigh, yrow)
    for k in range(count):
        o = first + k
        me = own_cell(o)
        cells = [ex * 5 + v for ex, v in near_all(o)]
        spread_columns(
            [dec[me, q : q + 1, :] for q in (OX, NY, NZ, ORHO2)] + [grad_psi[o : o + 1, :]], colb
        )
        gmsg = grad_message[o]
        for n, c in enumerate(cells):
            inner[n] = lax.dot_general(
                gmsg, cell_source(refs, c)[0:SLOTS, :], (((1,), (1,)), ((), ())),
                preferred_element_type=F32,
            )
        for r in range(0, SLOTS, CHUNK):
            sl = pl.ds(r, CHUNK)
            xi, yi, zi, ri2, gp = (colb[q, sl, :] for q in range(5))
            acc = None
            for n, c in enumerate(cells):
                dx = xi - dec[c, NX : NX + 1, :]
                dy = yi - dec[c, NY : NY + 1, :]
                dz = zi - dec[c, NZ : NZ + 1, :]
                s = dx * dx + dy * dy + dz * dz
                if n == 0:
                    s = s + self_far(r, CHUNK)
                m = jnp.maximum(1.0 - s, 0.0)
                inv = 1.0 / (s + dec[c, NR2 : NR2 + 1, :] + ri2)
                slope = dec[c, NR3 : NR3 + 1, :] * (inv * inv) * gp * (1.0 + m * inv)
                gauss = jnp.exp(-4.0 * s) * (1.0 + 2.0 * m) * inner[n, sl, :]
                rate = m * (slope + gauss)
                terms = [rate * dx, rate * dy, rate * dz]
                acc = terms if acc is None else [a + t for a, t in zip(acc, terms)]
                for d in range(3):
                    folded = fold8(terms[d])
                    if r == 0:
                        jacc[n, d] = folded
                    else:
                        jacc[n, d] += folded
            for d in range(3):
                keep_sum(pair, d, r, acc[d])
        for d in range(3):
            for n in range(len(cells)):
                out[k, d, n : n + 1, :] = jnp.sum(jacc[n, d], axis=0, keepdims=True)
            for n in range(len(cells), 9):
                out[k, d, n : n + 1, :] = jnp.zeros((1, SLOTS), F32)
            out[k, d, 9:10, :] = row_sum(pair, d)
            out[k, d, 10:16, :] = jnp.zeros((6, SLOTS), F32)


def gather_kernel(count, *refs):
    pieces, direct, core, edge = refs[: 8 // count], refs[-3], refs[-2], refs[-1]
    for ex in range(4):
        for v in range(5):
            for d in range(3):
                value = None
                for o in range(8):
                    near = near_all(o)
                    if (ex, v) not in near:
                        continue
                    n = near.index((ex, v))
                    term = pieces[o // count][o % count, d, n : n + 1, :]
                    value = term if value is None else value + term
                value = -4.0 * value
                if ex in (1, 2) and v < 4:
                    o = (ex - 1) * 4 + v
                    value = value - direct[d, o : o + 1, :]
                    value = value + 4.0 * pieces[o // count][o % count, d, 9:10, :]
                if v == 4:
                    edge[d * 4 + ex : d * 4 + ex + 1, :] = value
                else:
                    core[ex, d, v : v + 1, :] = value
    edge[12:16, :] = jnp.zeros((4, SLOTS), F32)


def weigh_kernel(slots, targets, sums, out):
    core = lax.axis_index("gy") % 2
    row = sums[SLOTS + 1 : SLOTS + 2, :]
    target = jnp.where(core == 0, targets[0], targets[1])
    weight = (row * (1.0 / slots) - target) * (1.0 / math.sqrt(slots))
    out[...] = sums[...] * weight
    out[SLOTS + 1 : SLOTS + 2, :] = row


def finish_kernel(slots, scaled, partner, stay, *refs):
    outs, staged, sem = refs[:5], refs[5:10], refs[10]
    energies, forces, grad_mix, grad_out, grad_scale = staged
    seat = lax.axis_index("gy")
    core, upper = seat % 2, seat // 2
    for d in range(3):
        for x in range(2):
            for y in range(2):
                row = upper if y == 0 else 1 - upper
                k = SLOTS + 8 + d * 4 + x * 2 + y
                forces[d, core, x, pl.ds(row, 1), :] = stay[d, x, pl.ds(y, 1), :]
                forces[d, 1 - core, x, pl.ds(row, 1), :] = partner[k : k + 1, :]
    grad_mix[...] = scaled[0:SLOTS, :] + partner[0:SLOTS, :]
    grad_out[...] = scaled[SLOTS : SLOTS + 1, :] + partner[SLOTS : SLOTS + 1, :]
    both = scaled[SLOTS + 2 : SLOTS + 3, :] + partner[SLOTS + 2 : SLOTS + 3, :]
    grad_scale[...] = both[:, 0:32]
    lane = lax.broadcasted_iota(jnp.int32, (1, SLOTS), 1)
    mine, theirs = scaled[SLOTS + 1 : SLOTS + 2, :], partner[SLOTS + 1 : SLOTS + 2, :]
    energies[...] = (jnp.where(lane == core, mine, theirs) * (1.0 / slots))[:, 0:2]
    copies = [pltpu.make_async_copy(a, b, sem.at[i]) for i, (a, b) in enumerate(zip(staged, outs))]
    for copy in copies:
        copy.start()
    for copy in copies:
        copy.wait()


def vmem(count):
    return [pl.BlockSpec(memory_space=pltpu.VMEM)] * count


def smem(count):
    return [pl.BlockSpec(memory_space=pltpu.SMEM)] * count


def shape(*dims, dtype=F32):
    return jax.ShapeDtypeStruct(dims, dtype)


def square(*lead, dtype=F32):
    return pltpu.VMEM(lead + (SLOTS, SLOTS), dtype)


def call(kernel, name, in_specs, out_shape, scratch, flops=1000000):
    single = not isinstance(out_shape, tuple)
    return pl.pallas_call(
        kernel,
        name=name,
        in_specs=in_specs,
        out_specs=vmem(1)[0] if single else tuple(vmem(len(out_shape))),
        out_shape=out_shape,
        scratch_shapes=scratch,
        compiler_params=pltpu.CompilerParams(vmem_limit_bytes=40 << 20),
        cost_estimate=pl.CostEstimate(flops=flops, transcendentals=0, bytes_accessed=1 << 20),
    )


def outward(value, axis):
    pairs = [(i, i + 1) for i in range(1, lax.axis_size(axis) - 1, 2)]
    return lax.ppermute(value, axis, pairs + [(j, i) for i, j in pairs])


def exchange(low, high, axis):
    even = lax.axis_index(axis) % 2 == 0
    outer = outward(jnp.where(even, low, high), axis)
    near = flip(jnp.where(even, high, low), axis, 1)
    return jnp.where(even, outer, near), jnp.where(even, near, outer)


def flip(value, axis, bit):
    return lax.ppermute(value, axis, [(i, i ^ bit) for i in range(lax.axis_size(axis))])


PIECE = 2


def on_device(
    positions, charges, slot_bead_types, cell_counts, features,
    radius_table, scale_table, mix_weight, out_weight, targets,
):
    total_slots = 2 * lax.axis_size("gx") * 2 * lax.axis_size("gy") * SLOTS
    seat = lax.axis_index("gy")
    core, upper = seat % 2, seat // 2
    inner = (core ^ upper) == 0
    half = shape(2, 2, ROWS, SLOTS, dtype=BF16)
    big = [
        pltpu.with_memory_space_constraint(v, pltpu.HBM)
        for v in (cell_counts, radius_table, scale_table, positions, charges, slot_bead_types, features, mix_weight,
                  out_weight.reshape(1, SLOTS))
    ]
    kept, sent, mix, outw, factor = call(
        pack_kernel, "pack", [pl.BlockSpec(memory_space=pltpu.HBM)] * 9,
        (half, half, shape(SLOTS, SLOTS, dtype=BF16), shape(1, SLOTS), shape(1, SLOTS)),
        [pltpu.SMEM((2, 2, 2), jnp.int32), pltpu.SMEM((32,), F32), pltpu.SMEM((32,), F32),
         pltpu.VMEM((3, 2, 2, 2, SLOTS), F32), pltpu.VMEM((2, 2, 2, SLOTS), F32),
         pltpu.VMEM((2, 2, 2, SLOTS), jnp.int32), square(2, 2, 2, dtype=BF16),
         pltpu.SemaphoreType.DMA((9,))],
        10000,
    )(*big)
    got = flip(sent, "gy", 1)
    low, high = (
        jnp.concatenate([jnp.where(inner, kept[x], got[x]), jnp.where(inner, got[x], kept[x])])
        for x in range(2)
    )

    xlow, xhigh = exchange(low, high, "gx")
    state = (shape(8, SLOTS, SLOTS), shape(8, 32, SLOTS), shape(8, 8, SLOTS))
    code, hots = shape(20, 16, SLOTS), shape(20, 32, SLOTS, dtype=BF16)
    started = call(
        first_own_kernel, "first_own", vmem(2), state,
        [pltpu.VMEM((8, 16, SLOTS), F32), pltpu.VMEM((8, 32, SLOTS), BF16), square(4),
         square(6, dtype=BF16), square(6, dtype=BF16), square(1, 2, dtype=BF16)],
    )(low, high)
    xlow, xhigh, low, high, started = lax.optimization_barrier((xlow, xhigh, low, high, started))
    yrow = flip(jnp.stack([xlow[3], low[3], high[3], xhigh[3]]), "gy", 2)
    dec, hot, *started = call(
        first_side_kernel, "first_side", vmem(7), (code, hots) + state,
        [square(4), square(5, dtype=BF16), square(5, dtype=BF16), square(1, 2, dtype=BF16)],
    )(xlow, low, high, xhigh, *started)
    dec, bead, act, message, parts = call(
        first_halo_kernel, "first_halo", vmem(8),
        (code, shape(4, 8, SLOTS), shape(8, SLOTS, SLOTS),
         shape(8, SLOTS, SLOTS, dtype=BF16), shape(8, 32, SLOTS)),
        [pltpu.VMEM((20, 32, SLOTS), BF16), square(4), square(5, dtype=BF16),
         square(5, dtype=BF16), square(2, 2, dtype=BF16), pltpu.VMEM((8, 8, SLOTS), F32)],
    )(dec, hot, yrow, *started, mix, outw)

    def second_own(side, dec, bead):
        return call(
            lambda *refs: second_own_kernel(side, *refs), f"second_own{side}", vmem(2),
            shape(4, 8, SLOTS),
            [square(5), square(5, 2, dtype=BF16), pltpu.VMEM((20, 8, SLOTS), F32)],
        )(dec, bead)

    born = bead[0]
    bxlow, bxhigh = exchange(born[0:4], born[4:8], "gx")
    sums0 = second_own(0, dec, bead)
    bxlow, bxhigh, bead, sums0 = lax.optimization_barrier((bxlow, bxhigh, bead, sums0))
    byrow = flip(jnp.stack([bxlow[3], born[3], born[7], bxhigh[3]]), "gy", 2)
    sums1 = second_own(1, dec, bead)

    grad_psi, grad_message, direct, sums = call(
        second_halo_kernel, "second_halo", vmem(13),
        (shape(8, SLOTS), shape(8, SLOTS, SLOTS, dtype=BF16), shape(3, 8, SLOTS),
         shape(SLOTS + 8, SLOTS)),
        [square(5), square(5, 2, dtype=BF16), pltpu.VMEM((20, 8, SLOTS), F32),
         pltpu.VMEM((8, 8, SLOTS), F32)],
    )(dec, bead, bxlow, bxhigh, byrow, sums0, sums1, act, message, parts, mix, outw, factor)

    def third(first, grad_psi):
        return call(
            lambda *refs: third_kernel(first, PIECE, *refs), f"third{first}", vmem(8),
            shape(PIECE, 3, 16, SLOTS),
            [square(5), square(3, 2, dtype=BF16), pltpu.VMEM((9, 3, 8, SLOTS), F32), square(9)],
        )(xlow, low, high, xhigh, yrow, dec, grad_psi, grad_message)

    bits = [1, 2, 4, 12, 16, 48]
    pieces = []
    for bit in bits[1:5]:
        other = flip(sums, "gx", bit)
        piece = third(PIECE * len(pieces), grad_psi)
        other, grad_psi, piece = lax.optimization_barrier((other, grad_psi, piece))
        pieces.append(piece)
        sums = sums + other
    block, edge = call(
        lambda *refs: gather_kernel(PIECE, *refs), "gather", vmem(8 // PIECE + 1),
        (shape(4, 3, 4, SLOTS), shape(16, SLOTS)), [],
    )(*pieces, direct)
    joint = jnp.concatenate([sums, edge])
    other = flip(joint, "gy", 2)
    sums = sums + other[: SLOTS + 8]
    block = block.at[:, :, 3].add(jnp.swapaxes(other[SLOTS + 8 : SLOTS + 20].reshape(3, 4, SLOTS), 0, 1))
    even = lax.axis_index("gx") % 2 == 0
    facing, away = jnp.where(even, block[3], block[0]), jnp.where(even, block[0], block[3])
    outer = outward(away, "gx")
    other = flip(jnp.concatenate([sums, facing.reshape(12, SLOTS)]), "gx", 1)
    sums = sums + other[: SLOTS + 8]
    near = other[SLOTS + 8 :].reshape(3, 4, SLOTS)
    for bit in bits[5:]:
        sums = sums + flip(sums, "gx", bit)
    own = jnp.stack(
        [block[1] + jnp.where(even, outer, near), block[2] + jnp.where(even, near, outer)], axis=1
    )
    own = own.reshape(3, 2, 2, 2, SLOTS)
    front, back = own[:, :, 0], own[:, :, 1]
    stay, leave = jnp.where(inner, front, back), jnp.where(inner, back, front)

    scaled = call(
        lambda *refs: weigh_kernel(total_slots, *refs), "weigh", smem(1) + vmem(1),
        shape(SLOTS + 8, SLOTS), [], 1000,
    )(targets, sums)
    partner = flip(jnp.concatenate([scaled, leave.reshape(12, SLOTS)]), "gy", 1)
    outs = (shape(1, 2), shape(3, 2, 2, 2, SLOTS), shape(SLOTS, SLOTS), shape(1, SLOTS), shape(1, 32))
    energies, forces, grad_mix, grad_out, grad_scale = pl.pallas_call(
        lambda *refs: finish_kernel(total_slots, *refs),
        name="finish",
        in_specs=vmem(3),
        out_specs=tuple([pl.BlockSpec(memory_space=pltpu.HBM)] * 5),
        out_shape=outs,
        scratch_shapes=[pltpu.VMEM(o.shape, F32) for o in outs] + [pltpu.SemaphoreType.DMA((5,))],
        compiler_params=pltpu.CompilerParams(vmem_limit_bytes=8 << 20),
    )(scaled, partner, stay)
    return (
        energies.reshape(2), forces, grad_mix, grad_out.reshape(SLOTS), grad_scale.reshape(32)
    )


def solution(mesh):
    placed = (
        P(None, None, "gx", "gy", None),
        P(None, "gx", "gy", None),
        P(None, "gx", "gy", None),
        P(None, "gx", "gy"),
        P(None, "gx", "gy", None, None),
        P(),
        P(),
        P(),
        P(),
        P(),
    )
    return jax.shard_map(
        on_device,
        mesh=mesh,
        in_specs=placed,
        out_specs=(P(), P(None, None, "gx", "gy", None), P(), P(), P()),
        check_vma=False,
    )
```

```python
import math

import jax
import jax.numpy as jnp
from jax import lax
from jax.experimental import pallas as pl
from jax.experimental.pallas import tpu as pltpu
from jax.sharding import PartitionSpec as P

SOLVENT = -0.5 * 0.98726
SCREEN_GAIN = 12.0
FAR = 4096.0
LOG2E = math.log2(math.e)
GAUSS = -4.0 * LOG2E
SLOTS = 128
ROWS = 144
CHUNK = 32
F32 = jnp.float32
BF16 = jnp.bfloat16


def split3(row):
    high = row.astype(BF16).astype(F32)
    rest = row - high
    mid = rest.astype(BF16).astype(F32)
    return [high, mid, rest - mid]


def pack_kernel(
    count_any, radius_any, scale_any, pos_any, charge_any, kind_any, feat_any, mix_any, outw_any,
    kept, sent, mix_out, outw_out, factor_out, table_out, counts, radius, scale, pos, charge, kind, feat, sem,
):
    copies = [
        pltpu.make_async_copy(src, dst, sem.at[i])
        for i, (src, dst) in enumerate(
            (
                (pos_any, pos),
                (charge_any, charge),
                (kind_any, kind),
                (feat_any, feat),
                (mix_any, mix_out),
                (outw_any, outw_out),
                (count_any, counts),
                (radius_any, radius),
                (scale_any, scale),
            )
        )
    ]
    for copy in copies:
        copy.start()
    for copy in copies:
        copy.wait()
    place = lax.axis_index("gy")
    core = place % 2
    upper = place // 2
    slot = lax.broadcasted_iota(jnp.int32, (1, SLOTS), 1)
    zero = jnp.zeros((1, SLOTS), F32)
    spots = [(s, x, y) for s in range(2) for x in range(2) for y in range(2)]

    def seat(s, y):
        frame = core if s == 0 else 1 - core
        row = upper if y == 0 else 1 - upper
        return frame, row

    found = []
    for s, x, y in spots:
        frame, row = seat(s, y)
        found.append(kind[frame, x, pl.ds(row, 1), :])
    kinds = jnp.concatenate(found, axis=0)
    rho = jnp.zeros((1, SLOTS), F32)
    factor = jnp.zeros((1, SLOTS), F32)
    for k in range(32):
        rho = jnp.where(slot == k, radius[k], rho)
        factor = jnp.where(slot == k, scale[k], factor)
    reach = rho * factor
    factor_out[...] = rho * reach * reach
    table = jnp.concatenate(split3(rho) + split3(reach) + [zero] * 10, axis=0)
    table_out[...] = table[:, 0:32].astype(BF16)
    for o, (s, x, y) in enumerate(spots):
        frame, row = seat(s, y)
        out = (kept, sent)[s]
        rows = []
        for d in range(3):
            rows += split3(pos[d, frame, x, pl.ds(row, 1), :])
        rows += split3(charge[frame, x, pl.ds(row, 1), :])
        rows.append(kinds[o : o + 1].astype(F32))
        rows.append((slot < counts[frame, x, row]).astype(F32))
        rows += [zero] * (16 - len(rows))
        out[x, y, 0:SLOTS, :] = feat[frame, x, row]
        out[x, y, SLOTS:ROWS, :] = jnp.concatenate(rows, axis=0).astype(BF16)


def chooser():
    r = lax.broadcasted_iota(jnp.int32, (16, 16), 0)
    k = lax.broadcasted_iota(jnp.int32, (16, 16), 1)
    triple = (r < 4) & (k >= 3 * r) & (k < 3 * r + 3)
    single = ((r == 4) | (r == 5)) & (k == r + 8)
    return jnp.where(triple | single, 1.0, 0.0).astype(BF16)


def near_rows(got, looked):
    valid = got[5:6] > 0.0
    rho = looked[0:1] + looked[1:2] + looked[2:3]
    reach = looked[3:4] + looked[4:5] + looked[5:6]
    square = reach * reach
    return [
        jnp.where(valid, got[0:1], -FAR),
        got[1:2],
        got[2:3],
        got[3:4],
        square,
        square * reach,
        rho,
        got[4:5],
        got[5:6],
        jnp.where(valid, got[0:1], FAR),
        rho * rho,
    ]


NX, NY, NZ, NQ, NR2, NR3, NRHO, NKIND, NVALID, OX, ORHO2 = range(11)


def spread_columns(rows, out):
    pad = [jnp.zeros((1, SLOTS), F32)] * (8 - len(rows))
    cols = jnp.transpose(jnp.concatenate(rows + pad, axis=0))
    for q in range(len(rows)):
        out[q] = jnp.broadcast_to(cols[:, q : q + 1], (SLOTS, SLOTS))


def self_far(start, size):
    r = lax.broadcasted_iota(jnp.int32, (size, SLOTS), 0) + start
    c = lax.broadcasted_iota(jnp.int32, (size, SLOTS), 1)
    return jnp.where(r == c, FAR * FAR, 0.0)


def keep_sum(pair, q, start, value):
    size = value.shape[0]
    high = value.astype(BF16)
    pair[q, 0, pl.ds(start, size), :] = high
    pair[q, 1, pl.ds(start, size), :] = (value - high.astype(F32)).astype(BF16)


def row_sum(pair, q):
    ones = jnp.ones((8, SLOTS), BF16)
    dims = (((1,), (1,)), ((), ()))
    high = lax.dot_general(ones, pair[q, 0], dims, preferred_element_type=F32)
    low = lax.dot_general(ones, pair[q, 1], dims, preferred_element_type=F32)
    return (high + low)[0:1]


def own_cell(o):
    return (o // 4 + 1) * 5 + o % 4


def near_own(o):
    x, v = o // 4, o % 4
    rows = [w for w in (v, v - 1, v + 1) if 0 <= w < 4]
    return [x * 4 + w for w in rows] + [(1 - x) * 4 + w for w in rows]


def near_halo(o):
    x, v = o // 4, o % 4
    cells = [15 * x + w for w in (v - 1, v, v + 1) if w >= 0]
    return cells + ([9, 14] if v == 3 else [])


def near_all(o):
    x, v = o // 4, o % 4
    spots = [(0, 0)] + [(p, q) for p in (-1, 0, 1) for q in (-1, 0, 1) if (p, q) != (0, 0)]
    return [(x + 1 + p, v + q) for p, q in spots if v + q >= 0]


def gather_rows(ref, q, count=8):
    return jnp.concatenate([ref[o, q : q + 1, :] for o in range(count)], axis=0)


def unpack(pick, table, coded, c, dec, hot):
    got = jnp.dot(pick, coded, preferred_element_type=F32)
    kinds = lax.broadcasted_iota(jnp.int32, (32, SLOTS), 0).astype(F32)
    match = jnp.where(kinds == got[4:5], 1.0, 0.0).astype(BF16)
    hot[c] = match
    looked = jnp.dot(table[...], match, preferred_element_type=F32)
    for q, row in enumerate(near_rows(got, looked)):
        dec[c, q : q + 1, :] = row


def first_blocks(cells, with_self, dec, feat, hot, colb, wgt, scl, pair, message, parts):
    size = CHUNK
    for r in range(0, SLOTS, size):
        sl = pl.ds(r, size)
        xi, yi, zi, ri2 = (colb[q, sl, :] for q in range(4))
        acc = None
        for n, c in enumerate(cells):
            rj2 = dec[c, NR2 : NR2 + 1, :]
            dx = xi - dec[c, NX : NX + 1, :]
            dy = yi - dec[c, NY : NY + 1, :]
            dz = zi - dec[c, NZ : NZ + 1, :]
            s = dx * dx + dy * dy + dz * dz
            if with_self and n == 0:
                s = s + self_far(r, size)
            m = jnp.maximum(1.0 - s, 0.0)
            t = m * m
            inv = 1.0 / (s + rj2 + ri2)
            ti = t * (inv * inv)
            term = ti * dec[c, NR3 : NR3 + 1, :]
            acc = term if acc is None else acc + term
            wgt[n, sl, :] = (t * jnp.exp2(s * GAUSS)).astype(BF16)
            scl[n, sl, :] = (ti * (3.0 - (4.0 * rj2) * inv)).astype(BF16)
        keep_sum(pair, 0, r, acc)
    for n, c in enumerate(cells):
        term = jnp.dot(wgt[n], feat(c), preferred_element_type=F32)
        part = lax.dot_general(
            hot[c], scl[n], (((1,), (1,)), ((), ())), preferred_element_type=F32
        )
        message = term if message is None else message + term
        parts = part if parts is None else parts + part
    return message, parts


def first_own_kernel(table, low, high, msg_out, part_out, scr_out, dec, hot, colb, wgt, scl, pair):
    pick = chooser()
    for x in range(2):
        for v in range(4):
            unpack(pick, table, (low, high)[x][v, SLOTS:ROWS, :], x * 4 + v, dec, hot)
    for o in range(8):
        spread_columns([dec[o, q : q + 1, :] for q in (OX, NY, NZ, ORHO2)], colb)
        message, parts = first_blocks(
            near_own(o), True, dec, lambda c: (low, high)[c // 4][c % 4, 0:SLOTS, :],
            hot, colb, wgt, scl, pair, None, None,
        )
        msg_out[o] = message
        part_out[o] = parts
        scr_out[o] = jnp.broadcast_to(row_sum(pair, 0), (8, SLOTS))


def cell_source(refs, c):
    ex, v = c // 5, c % 5
    return refs[4].at[ex] if v == 4 else refs[ex].at[v]


def first_side_kernel(
    table, xlow, low, high, xhigh, msg_in, part_in, scr_in,
    dec, hot, msg_out, part_out, scr_out, colb, wgt, scl, pair,
):
    pick = chooser()
    refs = (xlow, low, high, xhigh)
    for ex in range(4):
        for v in range(4):
            unpack(pick, table, refs[ex][v, SLOTS:ROWS, :], ex * 5 + v, dec, hot)
        dec[ex * 5 + 4] = jnp.zeros((16, SLOTS), F32)
        hot[ex * 5 + 4] = jnp.zeros((32, SLOTS), BF16)
    for o in range(8):
        me = own_cell(o)
        spread_columns([dec[me, q : q + 1, :] for q in (OX, NY, NZ, ORHO2)], colb)
        message, parts = first_blocks(
            [c for c in near_halo(o) if c % 5 != 4], False, dec,
            lambda c: refs[c // 5][c % 5, 0:SLOTS, :],
            hot, colb, wgt, scl, pair, msg_in[o], part_in[o],
        )
        msg_out[o] = message
        part_out[o] = parts
        scr_out[o] = scr_in[o] + row_sum(pair, 0)


def first_halo_kernel(
    table, dec_in, hot_in, yrow, msg_in, part_in, scr_in, mix, outw,
    dec, bead, act_out, msg_out, part_out, hot, colb, wgt, scl, pair, sums,
):
    pick = chooser()
    dec[...] = dec_in[...]
    hot[...] = hot_in[...]
    for ex in range(4):
        unpack(pick, table, yrow[ex, SLOTS:ROWS, :], ex * 5 + 4, dec, hot)
    weight = outw[...]
    for o in range(8):
        me = own_cell(o)
        message, parts = msg_in[o], part_in[o]
        screen = scr_in[o, 0:1, :]
        if o % 4 == 3:
            spread_columns([dec[me, q : q + 1, :] for q in (OX, NY, NZ, ORHO2)], colb)
            message, parts = first_blocks(
                [c for c in near_halo(o) if c % 5 == 4], False, dec,
                lambda c: yrow[c // 5, 0:SLOTS, :],
                hot, colb, wgt, scl, pair, message, parts,
            )
            screen = screen + row_sum(pair, 0)
        part_out[o] = parts
        message = message.astype(BF16)
        msg_out[o] = message
        act = jnp.tanh(jnp.dot(message, mix[...], preferred_element_type=F32))
        act_out[o] = act
        keep_sum(pair, 1, 0, act * weight)
        sums[o, 0:1, :] = screen
        sums[o, 1:2, :] = row_sum(pair, 1)
    cells = [own_cell(o) for o in range(8)]
    rho = jnp.concatenate([dec[c, NRHO : NRHO + 1, :] for c in cells], axis=0)
    valid = jnp.concatenate([dec[c, NVALID : NVALID + 1, :] for c in cells], axis=0)
    tanh_screen = jnp.tanh(SCREEN_GAIN * rho * gather_rows(sums, 0))
    tanh_corr = jnp.tanh(gather_rows(sums, 1))
    born = rho * (1.0 + 0.5 * tanh_corr) / (1.0 - 0.8 * tanh_screen)
    bead[0] = jnp.where(valid > 0.0, born, 1.0)
    bead[1] = tanh_screen
    bead[2] = tanh_corr
    bead[3] = rho


def second_blocks(cells, with_self, dec, born, colb, pair):
    size = CHUNK // 2
    for r in range(0, SLOTS, size):
        sl = pl.ds(r, size)
        xi, yi, zi, bi, ibi = (colb[q, sl, :] for q in range(5))
        acc = None
        for n, c in enumerate(cells):
            bj = born[c, 0:1, :]
            dx = xi - dec[c, NX : NX + 1, :]
            dy = yi - dec[c, NY : NY + 1, :]
            dz = zi - dec[c, NZ : NZ + 1, :]
            s = dx * dx + dy * dy + dz * dz
            if with_self and n == 0:
                s = s + self_far(r, size)
            m = jnp.maximum(1.0 - s, 0.0)
            arg = s * (ibi * born[c, 1:2, :])
            bg = bj * jnp.exp2(arg * -LOG2E)
            rinv = lax.rsqrt(s + bi * bg)
            mq = m * dec[c, NQ : NQ + 1, :] * rinv
            mi = m * (rinv * rinv)
            rate = mq * (2.0 + mi * (0.5 - bg * (0.125 * born[c, 1:2, :])))
            terms = [m * mq, (mq * mi) * (bg * (1.0 + arg)), rate * dx, rate * dy, rate * dz]
            acc = terms if acc is None else [a + t for a, t in zip(acc, terms)]
        for q in range(5):
            keep_sum(pair, q, r, acc[q])


def second_columns(me, dec, born, colb):
    spread_columns(
        [dec[me, q : q + 1, :] for q in (OX, NY, NZ)]
        + [born[me, 0:1, :], 0.25 * born[me, 1:2, :]],
        colb,
    )


def second_own_kernel(side, dec, bead, part, colb, pair, born):
    for o in range(8):
        c = own_cell(o)
        born[c, 0:1, :] = bead[0, o : o + 1, :]
        born[c, 1:2, :] = 1.0 / bead[0, o : o + 1, :]
    for v in range(4):
        o = side * 4 + v
        second_columns(own_cell(o), dec, born, colb)
        second_blocks([own_cell(p) for p in near_own(o)], True, dec, born, colb, pair)
        for q in range(5):
            part[v, q : q + 1, :] = row_sum(pair, q)


def second_halo_kernel(
    dec, bead, xlow, xhigh, yrow, part0, part1, act, message, parts, mix, outw, factor,
    grad_psi, grad_message, direct, mix_out, colb, pair, born, sums,
):
    for c in range(20):
        ex, v = c // 5, c % 5
        if v == 4:
            row = yrow[ex : ex + 1, :]
        elif ex in (1, 2):
            row = bead[0, (ex - 1) * 4 + v : (ex - 1) * 4 + v + 1, :]
        else:
            row = (xlow if ex == 0 else xhigh)[v : v + 1, :]
        row = jnp.where(dec[c, NVALID : NVALID + 1, :] > 0.0, row, 1.0)
        born[c, 0:1, :] = row
        born[c, 1:2, :] = 1.0 / row
    for o in range(8):
        second_columns(own_cell(o), dec, born, colb)
        second_blocks(near_halo(o), False, dec, born, colb, pair)
        before = (part0, part1)[o // 4]
        for q in range(5):
            sums[o, q : q + 1, :] = row_sum(pair, q) + before[o % 4, q : q + 1, :]
    total = [gather_rows(sums, q) for q in range(5)]
    cells = [own_cell(o) for o in range(8)]
    charge = jnp.concatenate([dec[c, NQ : NQ + 1, :] for c in cells], axis=0)
    valid = jnp.concatenate([dec[c, NVALID : NVALID + 1, :] for c in cells], axis=0)
    inv = 1.0 / bead[0]
    scaled = SOLVENT * charge
    self_energy = scaled * charge * valid * inv
    energy = scaled * total[0] + self_energy
    grad_born = -scaled * total[1] - self_energy * inv
    for d in range(3):
        direct[d] = -4.0 * scaled * total[2 + d]
    tanh_screen, tanh_corr, rho = bead[1], bead[2], bead[3]
    down = 1.0 - 0.8 * tanh_screen
    psi = (
        SCREEN_GAIN * rho * grad_born * rho * (1.0 + 0.5 * tanh_corr) * 0.8
        * (1.0 - tanh_screen * tanh_screen) / (down * down)
    )
    grad_psi[...] = psi
    grad_corr = grad_born * rho * 0.5 * (1.0 - tanh_corr * tanh_corr) / down
    corr_cols = jnp.transpose(grad_corr)
    weight = outw[...]
    kind = lax.broadcasted_iota(jnp.int32, (32, SLOTS), 0)
    lane = lax.broadcasted_iota(jnp.int32, (32, SLOTS), 1)
    mix_sum = None
    for o in range(8):
        col = corr_cols[:, o : o + 1]
        hidden = act[o]
        grad_hidden = (col * weight * (1.0 - hidden * hidden)).astype(BF16)
        grad_message[o] = lax.dot_general(
            grad_hidden, mix[...], (((1,), (1,)), ((), ())), preferred_element_type=F32
        ).astype(BF16)
        term = lax.dot_general(
            message[o], grad_hidden, (((0,), (0,)), ((), ())), preferred_element_type=F32
        )
        out_term = jnp.sum(col * hidden, axis=0, keepdims=True)
        scale_term = psi[o : o + 1] * parts[o]
        if mix_sum is None:
            mix_sum, out_sum, scale_sum = term, out_term, scale_term
        else:
            mix_sum = mix_sum + term
            out_sum = out_sum + out_term
            scale_sum = scale_sum + scale_term
    mix_out[0:SLOTS, :] = mix_sum
    both = jnp.sum(jnp.sum(energy, axis=0, keepdims=True), axis=1, keepdims=True)
    scale_col = jnp.sum(scale_sum, axis=1, keepdims=True)
    scale_row = jnp.sum(jnp.where(kind == lane, scale_col, 0.0), axis=0, keepdims=True)
    scale_row = scale_row * factor[...]
    mix_out[SLOTS:, :] = jnp.concatenate(
        [out_sum, jnp.broadcast_to(both, (1, SLOTS)), scale_row, jnp.zeros((5, SLOTS), F32)],
        axis=0,
    )


def fold8(value):
    total = value[0:8]
    for r in range(8, value.shape[0], 8):
        total = total + value[r : r + 8]
    return total


def third_kernel(
    first, count, xlow, low, high, xhigh, yrow, dec, grad_psi, grad_message,
    out, colb, pair, jacc, inner,
):
    refs = (xlow, low, high, xhigh, yrow)
    for k in range(count):
        o = first + k
        me = own_cell(o)
        cells = [ex * 5 + v for ex, v in near_all(o)]
        spread_columns(
            [dec[me, q : q + 1, :] for q in (OX, NY, NZ, ORHO2)] + [0.5 * grad_psi[o : o + 1, :]], colb
        )
        gmsg = grad_message[o]
        for n, c in enumerate(cells):
            inner[n] = lax.dot_general(
                gmsg, cell_source(refs, c)[0:SLOTS, :], (((1,), (1,)), ((), ())),
                preferred_element_type=F32,
            )
        for r in range(0, SLOTS, CHUNK):
            sl = pl.ds(r, CHUNK)
            xi, yi, zi, ri2, gp = (colb[q, sl, :] for q in range(5))
            acc = None
            for n, c in enumerate(cells):
                dx = xi - dec[c, NX : NX + 1, :]
                dy = yi - dec[c, NY : NY + 1, :]
                dz = zi - dec[c, NZ : NZ + 1, :]
                s = dx * dx + dy * dy + dz * dz
                if n == 0:
                    s = s + self_far(r, CHUNK)
                m = jnp.maximum(1.0 - s, 0.0)
                inv = 1.0 / (s + dec[c, NR2 : NR2 + 1, :] + ri2)
                slope = dec[c, NR3 : NR3 + 1, :] * (inv * inv) * gp * (1.0 + m * inv)
                gauss = jnp.exp2(s * GAUSS) * (0.5 + m) * inner[n, sl, :]
                rate = m * (slope + gauss)
                terms = [rate * dx, rate * dy, rate * dz]
                acc = terms if acc is None else [a + t for a, t in zip(acc, terms)]
                for d in range(3):
                    folded = fold8(terms[d])
                    if r == 0:
                        jacc[n, d] = folded
                    else:
                        jacc[n, d] += folded
            for d in range(3):
                keep_sum(pair, d, r, acc[d])
        for d in range(3):
            for n in range(len(cells)):
                out[k, d, n : n + 1, :] = jnp.sum(jacc[n, d], axis=0, keepdims=True)
            for n in range(len(cells), 9):
                out[k, d, n : n + 1, :] = jnp.zeros((1, SLOTS), F32)
            out[k, d, 9:10, :] = row_sum(pair, d)
            out[k, d, 10:16, :] = jnp.zeros((6, SLOTS), F32)


def gather_kernel(*refs):
    pieces, direct, core, edge = refs[:-3], refs[-3], refs[-2], refs[-1]
    seats = {}
    for piece, (_, first, count) in zip(pieces, PIECES):
        for k in range(count):
            seats[first + k] = (piece, k)
    for ex in range(4):
        for v in range(5):
            for d in range(3):
                value = None
                for o in range(8):
                    near = near_all(o)
                    if (ex, v) not in near:
                        continue
                    n = near.index((ex, v))
                    piece, k = seats[o]
                    term = piece[k, d, n : n + 1, :]
                    value = term if value is None else value + term
                value = -8.0 * value
                if ex in (1, 2) and v < 4:
                    o = (ex - 1) * 4 + v
                    value = value - direct[d, o : o + 1, :]
                    piece, k = seats[o]
                    value = value + 8.0 * piece[k, d, 9:10, :]
                if v == 4:
                    edge[d * 4 + ex : d * 4 + ex + 1, :] = value
                else:
                    core[ex, d, v : v + 1, :] = value
    edge[12:16, :] = jnp.zeros((4, SLOTS), F32)


def weigh_kernel(slots, targets, sums, out):
    core = lax.axis_index("gy") % 2
    row = sums[SLOTS + 1 : SLOTS + 2, :]
    target = jnp.where(core == 0, targets[0], targets[1])
    weight = (row * (1.0 / slots) - target) * (1.0 / math.sqrt(slots))
    out[...] = sums[...] * weight
    out[SLOTS + 1 : SLOTS + 2, :] = row


def finish_kernel(slots, scaled, partner, stay, *refs):
    outs, staged, sem = refs[:5], refs[5:10], refs[10]
    energies, forces, grad_mix, grad_out, grad_scale = staged
    seat = lax.axis_index("gy")
    core, upper = seat % 2, seat // 2
    for d in range(3):
        for x in range(2):
            for y in range(2):
                row = upper if y == 0 else 1 - upper
                k = SLOTS + 8 + d * 4 + x * 2 + y
                forces[d, core, x, pl.ds(row, 1), :] = stay[d, x, pl.ds(y, 1), :]
                forces[d, 1 - core, x, pl.ds(row, 1), :] = partner[k : k + 1, :]
    grad_mix[...] = scaled[0:SLOTS, :] + partner[0:SLOTS, :]
    grad_out[...] = scaled[SLOTS : SLOTS + 1, :] + partner[SLOTS : SLOTS + 1, :]
    both = scaled[SLOTS + 2 : SLOTS + 3, :] + partner[SLOTS + 2 : SLOTS + 3, :]
    grad_scale[...] = both[:, 0:32]
    lane = lax.broadcasted_iota(jnp.int32, (1, SLOTS), 1)
    mine, theirs = scaled[SLOTS + 1 : SLOTS + 2, :], partner[SLOTS + 1 : SLOTS + 2, :]
    energies[...] = (jnp.where(lane == core, mine, theirs) * (1.0 / slots))[:, 0:2]
    copies = [pltpu.make_async_copy(a, b, sem.at[i]) for i, (a, b) in enumerate(zip(staged, outs))]
    for copy in copies:
        copy.start()
    for copy in copies:
        copy.wait()


def vmem(count):
    return [pl.BlockSpec(memory_space=pltpu.VMEM)] * count


def smem(count):
    return [pl.BlockSpec(memory_space=pltpu.SMEM)] * count


def shape(*dims, dtype=F32):
    return jax.ShapeDtypeStruct(dims, dtype)


def square(*lead, dtype=F32):
    return pltpu.VMEM(lead + (SLOTS, SLOTS), dtype)


def call(kernel, name, in_specs, out_shape, scratch, flops=1000000):
    single = not isinstance(out_shape, tuple)
    return pl.pallas_call(
        kernel,
        name=name,
        in_specs=in_specs,
        out_specs=vmem(1)[0] if single else tuple(vmem(len(out_shape))),
        out_shape=out_shape,
        scratch_shapes=scratch,
        compiler_params=pltpu.CompilerParams(vmem_limit_bytes=40 << 20),
        cost_estimate=pl.CostEstimate(flops=flops, transcendentals=0, bytes_accessed=1 << 20),
    )


def outward(value, axis):
    pairs = [(i, i + 1) for i in range(1, lax.axis_size(axis) - 1, 2)]
    return lax.ppermute(value, axis, pairs + [(j, i) for i, j in pairs])


def exchange(low, high, axis):
    even = lax.axis_index(axis) % 2 == 0
    outer = outward(jnp.where(even, low, high), axis)
    near = flip(jnp.where(even, high, low), axis, 1)
    return jnp.where(even, outer, near), jnp.where(even, near, outer)


def flip(value, axis, bit):
    return lax.ppermute(value, axis, [(i, i ^ bit) for i in range(lax.axis_size(axis))])


PIECES = ((4, 0, 2), (12, 2, 3), (16, 5, 3))


def on_device(
    positions, charges, slot_bead_types, cell_counts, features,
    radius_table, scale_table, mix_weight, out_weight, targets,
):
    total_slots = 2 * lax.axis_size("gx") * 2 * lax.axis_size("gy") * SLOTS
    seat = lax.axis_index("gy")
    core, upper = seat % 2, seat // 2
    inner = (core ^ upper) == 0
    half = shape(2, 2, ROWS, SLOTS, dtype=BF16)
    big = [
        pltpu.with_memory_space_constraint(v, pltpu.HBM)
        for v in (cell_counts, radius_table, scale_table, positions, charges, slot_bead_types, features, mix_weight,
                  out_weight.reshape(1, SLOTS))
    ]
    kept, sent, mix, outw, factor, table = call(
        pack_kernel, "pack", [pl.BlockSpec(memory_space=pltpu.HBM)] * 9,
        (half, half, shape(SLOTS, SLOTS, dtype=BF16), shape(1, SLOTS), shape(1, SLOTS),
         shape(16, 32, dtype=BF16)),
        [pltpu.SMEM((2, 2, 2), jnp.int32), pltpu.SMEM((32,), F32), pltpu.SMEM((32,), F32),
         pltpu.VMEM((3, 2, 2, 2, SLOTS), F32), pltpu.VMEM((2, 2, 2, SLOTS), F32),
         pltpu.VMEM((2, 2, 2, SLOTS), jnp.int32), square(2, 2, 2, dtype=BF16),
         pltpu.SemaphoreType.DMA((9,))],
        10000,
    )(*big)
    got = flip(sent, "gy", 1)
    low, high = (
        jnp.concatenate([jnp.where(inner, kept[x], got[x]), jnp.where(inner, got[x], kept[x])])
        for x in range(2)
    )

    xlow, xhigh = exchange(low, high, "gx")
    state = (shape(8, SLOTS, SLOTS), shape(8, 32, SLOTS), shape(8, 8, SLOTS))
    code, hots = shape(20, 16, SLOTS), shape(20, 32, SLOTS, dtype=BF16)
    started = call(
        first_own_kernel, "first_own", vmem(3), state,
        [pltpu.VMEM((8, 16, SLOTS), F32), pltpu.VMEM((8, 32, SLOTS), BF16), square(4),
         square(6, dtype=BF16), square(6, dtype=BF16), square(1, 2, dtype=BF16)],
    )(table, low, high)
    xlow, xhigh, low, high, started = lax.optimization_barrier((xlow, xhigh, low, high, started))
    yrow = flip(jnp.stack([xlow[3], low[3], high[3], xhigh[3]]), "gy", 2)
    dec, hot, *started = call(
        first_side_kernel, "first_side", vmem(8), (code, hots) + state,
        [square(4), square(5, dtype=BF16), square(5, dtype=BF16), square(1, 2, dtype=BF16)],
    )(table, xlow, low, high, xhigh, *started)
    dec, bead, act, message, parts = call(
        first_halo_kernel, "first_halo", vmem(9),
        (code, shape(4, 8, SLOTS), shape(8, SLOTS, SLOTS),
         shape(8, SLOTS, SLOTS, dtype=BF16), shape(8, 32, SLOTS)),
        [pltpu.VMEM((20, 32, SLOTS), BF16), square(4), square(5, dtype=BF16),
         square(5, dtype=BF16), square(2, 2, dtype=BF16), pltpu.VMEM((8, 8, SLOTS), F32)],
    )(table, dec, hot, yrow, *started, mix, outw)

    def second_own(side, dec, bead):
        return call(
            lambda *refs: second_own_kernel(side, *refs), f"second_own{side}", vmem(2),
            shape(4, 8, SLOTS),
            [square(5), square(5, 2, dtype=BF16), pltpu.VMEM((20, 8, SLOTS), F32)],
        )(dec, bead)

    born = bead[0]
    bxlow, bxhigh = exchange(born[0:4], born[4:8], "gx")
    sums0 = second_own(0, dec, bead)
    bxlow, bxhigh, bead, sums0 = lax.optimization_barrier((bxlow, bxhigh, bead, sums0))
    byrow = flip(jnp.stack([bxlow[3], born[3], born[7], bxhigh[3]]), "gy", 2)
    sums1 = second_own(1, dec, bead)

    grad_psi, grad_message, direct, sums = call(
        second_halo_kernel, "second_halo", vmem(13),
        (shape(8, SLOTS), shape(8, SLOTS, SLOTS, dtype=BF16), shape(3, 8, SLOTS),
         shape(SLOTS + 8, SLOTS)),
        [square(5), square(5, 2, dtype=BF16), pltpu.VMEM((20, 8, SLOTS), F32),
         pltpu.VMEM((8, 8, SLOTS), F32)],
    )(dec, bead, bxlow, bxhigh, byrow, sums0, sums1, act, message, parts, mix, outw, factor)

    def third(first, count, grad_psi):
        return call(
            lambda *refs: third_kernel(first, count, *refs), f"third{first}", vmem(8),
            shape(count, 3, 16, SLOTS),
            [square(5), square(3, 2, dtype=BF16), pltpu.VMEM((9, 3, 8, SLOTS), F32), square(9)],
        )(xlow, low, high, xhigh, yrow, dec, grad_psi, grad_message)

    bits = [1, 2, 4, 12, 16, 48]
    pieces = []
    sums = sums + flip(sums, "gx", bits[1])
    for bit, first, count in PIECES:
        other = flip(sums, "gx", bit)
        piece = third(first, count, grad_psi)
        other, grad_psi, piece = lax.optimization_barrier((other, grad_psi, piece))
        pieces.append(piece)
        sums = sums + other
    block, edge = call(
        gather_kernel, "gather", vmem(len(PIECES) + 1),
        (shape(4, 3, 4, SLOTS), shape(16, SLOTS)), [],
    )(*pieces, direct)
    joint = jnp.concatenate([sums, edge])
    other = flip(joint, "gy", 2)
    sums = sums + other[: SLOTS + 8]
    block = block.at[:, :, 3].add(jnp.swapaxes(other[SLOTS + 8 : SLOTS + 20].reshape(3, 4, SLOTS), 0, 1))
    even = lax.axis_index("gx") % 2 == 0
    facing, away = jnp.where(even, block[3], block[0]), jnp.where(even, block[0], block[3])
    outer = outward(away, "gx")
    other = flip(jnp.concatenate([sums, facing.reshape(12, SLOTS)]), "gx", 1)
    sums = sums + other[: SLOTS + 8]
    near = other[SLOTS + 8 :].reshape(3, 4, SLOTS)
    for bit in bits[5:]:
        sums = sums + flip(sums, "gx", bit)
    own = jnp.stack(
        [block[1] + jnp.where(even, outer, near), block[2] + jnp.where(even, near, outer)], axis=1
    )
    own = own.reshape(3, 2, 2, 2, SLOTS)
    front, back = own[:, :, 0], own[:, :, 1]
    stay, leave = jnp.where(inner, front, back), jnp.where(inner, back, front)

    scaled = call(
        lambda *refs: weigh_kernel(total_slots, *refs), "weigh", smem(1) + vmem(1),
        shape(SLOTS + 8, SLOTS), [], 1000,
    )(targets, sums)
    partner = flip(jnp.concatenate([scaled, leave.reshape(12, SLOTS)]), "gy", 1)
    outs = (shape(1, 2), shape(3, 2, 2, 2, SLOTS), shape(SLOTS, SLOTS), shape(1, SLOTS), shape(1, 32))
    energies, forces, grad_mix, grad_out, grad_scale = pl.pallas_call(
        lambda *refs: finish_kernel(total_slots, *refs),
        name="finish",
        in_specs=vmem(3),
        out_specs=tuple([pl.BlockSpec(memory_space=pltpu.HBM)] * 5),
        out_shape=outs,
        scratch_shapes=[pltpu.VMEM(o.shape, F32) for o in outs] + [pltpu.SemaphoreType.DMA((5,))],
        compiler_params=pltpu.CompilerParams(vmem_limit_bytes=8 << 20),
    )(scaled, partner, stay)
    return (
        energies.reshape(2), forces, grad_mix, grad_out.reshape(SLOTS), grad_scale.reshape(32)
    )


def solution(mesh):
    placed = (
        P(None, None, "gx", "gy", None),
        P(None, "gx", "gy", None),
        P(None, "gx", "gy", None),
        P(None, "gx", "gy"),
        P(None, "gx", "gy", None, None),
        P(),
        P(),
        P(),
        P(),
        P(),
    )
    return jax.shard_map(
        on_device,
        mesh=mesh,
        in_specs=placed,
        out_specs=(P(), P(None, None, "gx", "gy", None), P(), P(), P()),
        check_vma=False,
    )
```
